32 devices in a mesh: dp: 16 (over z, y, x), seq: 2 (over core).
Axes of the slice: x: 2, y: 2, z: 4, core: 2. Of those that a mesh axis runs over, the one named last changes fastest.
Arguments:
- tokens: bfloat16 [16, 1024, 1024], P('dp', 'seq'), may hold values from -6 to 6
- segments: int32 [16, 1024], P('dp'), may hold values from 0 to 2, never falling along the last dimension, each value on 1 to 512 neighbouring positions
- cotangent: bfloat16 [16, 1024, 1024], P('dp', 'seq'), may hold values from -6 to 6
- query_weight: bfloat16 [1024, 1024], P(('dp', 'seq')), may hold values from -0.1875 to 0.1875
- key_weight: bfloat16 [1024, 1024], P(('dp', 'seq')), may hold values from -0.1875 to 0.1875
- value_weight: bfloat16 [1024, 1024], P(('dp', 'seq')), may hold values from -0.1875 to 0.1875
- out_weight: bfloat16 [1024, 1024], P(('dp', 'seq')), may hold values from -1.5 to 1.5
- up_weight: bfloat16 [1024, 4096], P(('dp', 'seq')), may hold values from -0.1875 to 0.1875
- down_weight: bfloat16 [4096, 1024], P(('dp', 'seq')), may hold values from -0.09375 to 0.09375
- query_bias: bfloat16 [1024], P(('dp', 'seq')), may hold values from -3 to 3
- value_bias: bfloat16 [1024], P(('dp', 'seq')), may hold values from -3 to 3
- out_bias: bfloat16 [1024], P(('dp', 'seq')), may hold values from -3 to 3
- up_bias: bfloat16 [4096], P(('dp', 'seq')), may hold values from -3 to 3
- down_bias: bfloat16 [1024], P(('dp', 'seq')), may hold values from -3 to 3
- first_gain: bfloat16 [1024], P(('dp', 'seq')), may hold values from 0.5 to 1.5
- first_shift: bfloat16 [1024], P(('dp', 'seq')), may hold values from -2 to 2
- second_gain: bfloat16 [1024], P(('dp', 'seq')), may hold values from 0.5 to 1.5
- second_shift: bfloat16 [1024], P(('dp', 'seq')), may hold values from -2 to 2
Outputs:
- output: bfloat16 [16, 1024, 1024], P('dp', 'seq')
- input_grad: float32 [16, 1024, 1024], P('dp', 'seq')
- query_weight_grad: float32 [1024, 1024], P(('dp', 'seq'))
- key_weight_grad: float32 [1024, 1024], P(('dp', 'seq'))
- value_weight_grad: float32 [1024, 1024], P(('dp', 'seq'))
- out_weight_grad: float32 [1024, 1024], P(('dp', 'seq'))
- up_weight_grad: float32 [1024, 4096], P(('dp', 'seq'))
- down_weight_grad: float32 [4096, 1024], P(('dp', 'seq'))
- query_bias_grad: float32 [1024], P(('dp', 'seq'))
- value_bias_grad: float32 [1024], P(('dp', 'seq'))
- out_bias_grad: float32 [1024], P(('dp', 'seq'))
- up_bias_grad: float32 [4096], P(('dp', 'seq'))
- down_bias_grad: float32 [1024], P(('dp', 'seq'))
- first_gain_grad: float32 [1024], P(('dp', 'seq'))
- first_shift_grad: float32 [1024], P(('dp', 'seq'))
- second_gain_grad: float32 [1024], P(('dp', 'seq'))
- second_shift_grad: float32 [1024], P(('dp', 'seq'))
The draws below stay inside these ranges and needn't reach their ends.
Inputs may be any that keep to these rules, and one draw needn't show every extreme that they name: `segments`: document numbers never fall along a sequence; documents are 1 to 512 tokens long.
All inputs are finite; a program needn't handle non-finite values.
Results may differ from the reference program's by a relative error of at most 0.011.
Values may be sent and summed in bfloat16 or wider, within the bound.
No kernel may reach another device: no remote copies, remote signals or barrier semaphores. Data moves between devices by JAX's collectives and lax.ppermute only.
A program may use at most 192 MiB of HBM per device.

```python
import math
import jax
import jax.numpy as jnp
import numpy as np
from jax import lax

D = 1024
HEADS = 16
HEAD_DIM = 64
FF = 4096
LEN = 1024
SEQS = 16


def levels(stream_key, extent, split, low, top_value):
    def one(dim, parts):
        draws = jax.random.uniform(jax.random.fold_in(jax.random.fold_in(stream_key, 6), dim), (parts,), jnp.float32, low / len(split), top_value / len(split))
        return jnp.repeat(jnp.exp(draws), extent[dim] // parts).reshape((-1,) + (1,) * (len(extent) - dim - 1))

    factor_of = one(*split[0])
    for cut in split[1:]:
        factor_of = factor_of * one(*cut)
    return factor_of


def profile(count, total, reach, skew):
    weights = [(1 << 20) // math.isqrt(rank ** skew) + 1 for rank in range(2, count + 1)]
    surplus, holding = total - reach - (count - 1), [1] * (count - 1)
    while surplus > 0:
        movable = [i for i in range(count - 1) if holding[i] < reach]
        mass, left = sum([weights[i] for i in movable]), surplus
        for i in movable:
            extra = min(reach - holding[i], max(1, left * weights[i] // mass), surplus)
            holding[i] = holding[i] + extra
            surplus = surplus - extra
    return np.array([reach] + holding)


def ragged_sizes(own_key, amount, total, bound, lean):
    if amount == 2:
        one = jax.random.randint(own_key, (), max(1, total - bound), min(bound, total - 1) + 1)
        return jnp.stack([one, total - one])
    lengths = jnp.asarray(profile(amount, total, bound, lean), jnp.int32)
    twos = (amount - 1) // 2
    giver, receiver = lengths[1:1 + 2 * twos:2], lengths[2:2 + 2 * twos:2]
    slack = jnp.minimum(giver - 1, bound - receiver)
    shifted = jax.random.randint(jax.random.fold_in(own_key, 1), (twos,), 0, 1 << 20) % (slack + 1)
    lengths = lengths.at[1:1 + 2 * twos:2].set(giver - shifted).at[2:2 + 2 * twos:2].set(receiver + shifted)
    return lengths[jax.random.permutation(jax.random.fold_in(own_key, 2), amount)]


def normal_values(own_key, shape, width, limit, split=(), held_as=jnp.bfloat16):
    values = width * jax.random.normal(own_key, shape, jnp.float32)
    if split:
        values = values * levels(own_key, shape, split, -0.22, 0.18)
    return jnp.clip(values, -limit, limit).astype(held_as)


def setup_inputs(seed: int = 0) -> dict:
    seeds = jax.random.split(jax.random.key(seed), 19)
    return {
        "tokens": normal_values(seeds[0], (SEQS, LEN, D), 1.0, 6.0, ((0, 16), (1, 2))),
        "segments": jax.vmap(lambda own: jnp.searchsorted(jnp.cumsum(ragged_sizes(own, 3, LEN, LEN // 2, 2)), jnp.arange(LEN), side="right"))(jax.random.split(seeds[1], SEQS)).reshape((SEQS, LEN)).astype(jnp.int32),
        "cotangent": normal_values(seeds[2], (SEQS, LEN, D), 1.0, 6.0, ((0, 16), (1, 2))),
        "query_weight": normal_values(seeds[3], (D, D), D ** -0.5, 0.1875, ((0, 32),)),
        "key_weight": normal_values(seeds[4], (D, D), D ** -0.5, 0.1875, ((0, 32),)),
        "value_weight": normal_values(seeds[5], (D, D), D ** -0.5, 0.1875, ((0, 32),)),
        "out_weight": normal_values(seeds[6], (D, D), (D // 64) ** -0.5, 1.5, ((0, 32),)),
        "up_weight": normal_values(seeds[7], (D, FF), D ** -0.5, 0.1875, ((0, 32),)),
        "down_weight": normal_values(seeds[8], (FF, D), FF ** -0.5, 0.09375, ((0, 32),)),
        "query_bias": normal_values(seeds[9], (D,), 0.5, 3.0, ((0, 32),)),
        "value_bias": normal_values(seeds[10], (D,), 0.5, 3.0, ((0, 32),)),
        "out_bias": normal_values(seeds[11], (D,), 0.5, 3.0, ((0, 32),)),
        "up_bias": normal_values(seeds[12], (FF,), 0.5, 3.0, ((0, 32),)),
        "down_bias": normal_values(seeds[13], (D,), 0.5, 3.0, ((0, 32),)),
        "first_gain": jnp.clip(1.0 + 0.1 * jax.random.normal(seeds[14], (D,), jnp.float32), 0.5, 1.5).astype(jnp.bfloat16),
        "first_shift": normal_values(seeds[15], (D,), 0.3, 2.0, ((0, 32),)),
        "second_gain": jnp.clip(1.0 + 0.1 * jax.random.normal(seeds[16], (D,), jnp.float32), 0.5, 1.5).astype(jnp.bfloat16),
        "second_shift": normal_values(seeds[17], (D,), 0.3, 2.0, ((0, 32),)),
    }


@jax.custom_vjp
def low(v):
    return lax.optimization_barrier(v.astype(jnp.bfloat16)).astype(jnp.float32)

@jax.custom_vjp
def low_back(v):
    return v

def low_keep(v):
    return (low(v), None)

def low_pass(kept, grad):
    return (grad,)

def back_keep(v):
    return (v, None)

def back_low(kept, grad):
    return (low(grad),)
low.defvjp(low_keep, low_pass)
low_back.defvjp(back_keep, back_low)
EPS = 1e-05
MASKED = -1000000000.0
HIGH = lax.Precision.HIGHEST

def layer_norm(matrix, norm_gain, norm_shift):
    row_mean = lax.optimization_barrier(jnp.mean(matrix, axis=-1, keepdims=True))
    centred = matrix - row_mean
    spread = lax.optimization_barrier(jnp.mean(centred * centred, axis=-1, keepdims=True))
    return centred * lax.rsqrt(spread + EPS) * norm_gain + norm_shift

def matmul(left, right):
    return jnp.dot(left, right, precision=HIGH)

def forward(block_tokens, block_segments, params):
    query_weight, key_weight, value_weight, out_weight, up_weight, down_weight, query_bias, value_bias, out_bias, up_bias, down_bias, first_gain, first_shift, second_gain, second_shift = params
    group_count, length, model_width = block_tokens.shape
    inputs = block_tokens.reshape(group_count * length, model_width)
    first_low = low(layer_norm(inputs, first_gain, first_shift))
    queries = low_back(low(matmul(first_low, query_weight) + query_bias))
    keys = low_back(low(matmul(first_low, key_weight)))
    values = low_back(low(matmul(first_low, value_weight) + value_bias))
    queries = queries.reshape(group_count, length, HEADS, HEAD_DIM)
    keys = keys.reshape(group_count, length, HEADS, HEAD_DIM)
    values = values.reshape(group_count, length, HEADS, HEAD_DIM)
    slopes = 2.0 ** (-8.0 * (jnp.arange(HEADS, dtype=jnp.float32) + 1.0) / HEADS)
    positions = jnp.arange(length, dtype=jnp.int32)
    offsets = (positions[:, None] - positions[None, :]).astype(jnp.float32)
    allowed = (positions[:, None] >= positions[None, :])[None, None] & (block_segments[:, None, :, None] == block_segments[:, None, None, :])
    scores = jnp.einsum('gihd,gjhd->ghij', queries, keys, precision=HIGH) * HEAD_DIM ** (-0.5)
    scores = scores - slopes[None, :, None, None] * offsets[None, None]
    scores = low_back(jnp.where(allowed, scores, MASKED))
    shares = low(jax.nn.softmax(scores, axis=-1))
    mixed = jnp.einsum('ghij,gjhd->gihd', shares, values, precision=HIGH)
    mixed = low_back(low(mixed.reshape(group_count * length, model_width)))
    attended = low_back(matmul(mixed, out_weight) + out_bias)
    middle = inputs + attended
    second_low = low(layer_norm(middle, second_gain, second_shift))
    hidden_pre = low_back(matmul(second_low, up_weight) + up_bias)
    activated = low(jax.nn.gelu(hidden_pre, approximate=True))
    down_out = low_back(matmul(activated, down_weight) + down_bias)
    result = middle + down_out
    return result.reshape(group_count, length, model_width)

def reference(tokens, segments, cotangent, query_weight, key_weight, value_weight, out_weight, up_weight, down_weight, query_bias, value_bias, out_bias, up_bias, down_bias, first_gain, first_shift, second_gain, second_shift):
    params = tuple((p.astype(jnp.float32) for p in (query_weight, key_weight, value_weight, out_weight, up_weight, down_weight, query_bias, value_bias, out_bias, up_bias, down_bias, first_gain, first_shift, second_gain, second_shift)))
    group_size = math.gcd(SEQS, max(1, 4096 // LEN))
    blocks = SEQS // group_size
    all_tokens = tokens.astype(jnp.float32).reshape(blocks, group_size, LEN, D)
    all_segments = segments.reshape(blocks, group_size, LEN)
    all_cotangent = cotangent.astype(jnp.float32).reshape(blocks, group_size, LEN, D)

    def scan_step(carried, block):
        block_tokens, block_segments, block_cotangent = block

        def forward_of(inputs, weights):
            return forward(inputs, block_segments, weights)
        result, pullback = jax.vjp(forward_of, block_tokens, params)
        grad_inputs, grad_params = pullback(block_cotangent)
        carried = jax.tree.map(jnp.add, carried, grad_params)
        return (carried, (result.astype(jnp.bfloat16), grad_inputs))
    zeros = jax.tree.map(jnp.zeros_like, params)
    grads, (results, grad_inputs) = lax.scan(scan_step, zeros, (all_tokens, all_segments, all_cotangent))
    return (results.reshape(SEQS, LEN, D), grad_inputs.reshape(SEQS, LEN, D), grads[0], grads[1], grads[2], grads[3], grads[4], grads[5], grads[6], grads[7], grads[8], grads[9], grads[10], grads[11], grads[12], grads[13], grads[14])
```

```python
import functools

import jax
import jax.numpy as jnp
from jax import lax
from jax.experimental import pallas as pl
from jax.experimental.pallas import tpu as pltpu
from jax.sharding import PartitionSpec as P


HEADS = 16
HEAD_DIM = 64
EPS = 1e-05
FAR = 1e30
BLOCK = 256
REACH = 512
BF = jnp.bfloat16
F32 = jnp.float32


def dot(left, right, contract):
    return lax.dot_general(left, right, (contract, ((), ())), preferred_element_type=F32)


def matmul(left, right):
    return dot(left, right, ((1,), (0,)))


def pick(array, index, axis):
    return lax.dynamic_index_in_dim(array, index, axis, keepdims=False)


def trade(array):
    return lax.ppermute(array, "seq", [(0, 1), (1, 0)])


def seq_gather(block, seq):
    if seq == 2:
        other = trade(block)
        first = lax.axis_index("seq") == 0
        return jnp.where(first, jnp.stack([block, other]), jnp.stack([other, block]))
    return lax.all_gather(block, "seq", axis=0)


def seq_columns(block, seq):
    if seq == 2:
        other = trade(block)
        first = lax.axis_index("seq") == 0
        return jnp.where(
            first,
            jnp.concatenate([block, other], axis=1),
            jnp.concatenate([other, block], axis=1),
        )
    return lax.all_gather(block, "seq", axis=1, tiled=True)


def seq_swap(blocks, seq):
    if seq == 2:
        me = lax.axis_index("seq")
        own, other = pick(blocks, me, 0), trade(pick(blocks, 1 - me, 0))
        return jnp.where(me == 0, jnp.stack([own, other]), jnp.stack([other, own]))
    return lax.all_to_all(blocks, "seq", 0, 0)


def seq_reduce(blocks, seq, send):
    if seq == 2:
        me = lax.axis_index("seq")
        other = trade(pick(blocks, 1 - me, 0).astype(send))
        return pick(blocks, me, 0).astype(F32) + other.astype(F32)
    return lax.psum_scatter(blocks.astype(F32), "seq", scatter_dimension=0, tiled=False)


def seq_total(partial, seq, send):
    if seq == 2:
        return partial + trade(partial.astype(send)).astype(F32)
    return lax.psum(partial, "seq")


def flip(array, bits, count):
    return lax.ppermute(array, "dp", [(i, i ^ bits) for i in range(count)])


def boxed(count):
    return count >= 4 and not count & (count - 1)


def place_kernel(widths, me_ref, *refs):
    near, got = (refs[0], refs[2]), (refs[1], refs[3])
    outs = refs[4:]
    me = me_ref[0]
    coords = (me % 2, (me // 2) % 2)
    for colour in range(2):
        for piece, late in ((near[colour], 0), (got[colour], 1)):
            for early in range(2):
                flips = (early, late) if colour == 0 else (late, early)
                low, side = coords[0] ^ flips[0], coords[1] ^ flips[1]
                start = 0
                for out, width in zip(outs, widths):
                    half = width // 2
                    out[0, side, low, :, colour * half : (colour + 1) * half] = piece[
                        early, 0, :, start : start + half
                    ]
                    start += half


def gather_blocks(blocks, count, after=None):
    rows, widths = blocks[0].shape[0], [b.shape[1] for b in blocks]
    if not boxed(count) or any(w % 256 for w in widths):
        return [lax.all_gather(b, "dp", axis=0, tiled=True) for b in blocks], blocks[0]
    n_far, half = count // 4, sum(widths) // 2
    block = jnp.concatenate([b[:, : w // 2] for b, w in zip(blocks, widths)]
                            + [b[:, w // 2 :] for b, w in zip(blocks, widths)], axis=1)
    if after is not None:
        block, _ = lax.optimization_barrier((block, after))
    slots = [block] + [flip(block, 4 * k, count) for k in range(1, n_far)]
    pieces = []
    for colour in range(2):
        far = jnp.stack([slot[:, colour * half : (colour + 1) * half] for slot in slots])
        first, second = (1, 2) if colour == 0 else (2, 1)
        near = jnp.stack([far, flip(far, first, count)])
        pieces += [near, flip(near, second, count)]
    out_specs = [
        pl.BlockSpec((1, 2, 2, rows, w), lambda k, me: ((me[0] // 4) ^ k, 0, 0, 0, 0))
        for w in widths
    ]
    outs = pl.pallas_call(
        functools.partial(place_kernel, widths),
        grid_spec=pltpu.PrefetchScalarGridSpec(
            num_scalar_prefetch=1,
            grid=(n_far,),
            in_specs=[pl.BlockSpec((2, 1, rows, half), lambda k, me: (0, k, 0, 0))] * 4,
            out_specs=out_specs,
        ),
        out_shape=[jax.ShapeDtypeStruct((n_far, 2, 2, rows, w), block.dtype) for w in widths],
    )(lax.axis_index("dp").astype(jnp.int32)[None], *pieces)
    return [out.reshape(count * rows, w) for out, w in zip(outs, widths)], slots[-1]


def gather_small(block, count):
    if not boxed(count):
        return lax.all_gather(block, "dp", axis=0)
    slots = jnp.stack([block] + [flip(block, 4 * k, count) for k in range(1, count // 4)])
    near = jnp.stack([slots, flip(slots, 2, count)], 1)
    whole = jnp.stack([near, flip(near, 1, count)], 2)
    whole = whole.reshape((count,) + block.shape).astype(F32)
    ids = jnp.arange(count)
    order = ((ids[:, None] ^ lax.axis_index("dp")) == ids[None, :]).astype(F32)
    return jnp.sum(order.reshape(count, count, 1, 1) * whole[None], axis=1)


def add_low(a, b):
    return (a.astype(F32) + b.astype(F32)).astype(b.dtype)


def scatter_near(grads, count, colour):
    me = lax.axis_index("dp")
    side, low = (me // 2) % 2, me % 2
    box = grads.reshape((count // 4, 2, 2) + grads.shape[1:])
    if colour == 0:
        order = ((1, 2, side), (1, 1, low))
    else:
        order = ((2, 1, low), (1, 2, side))
    for axis, bit, mine in order:
        got = flip(pick(box, 1 - mine, axis), bit, count)
        box = add_low(pick(box, mine, axis), got)
    return box


def scatter_far(box, count):
    far = lax.axis_index("dp") // 4
    total = pick(box, far, 0).astype(F32)
    for k in range(1, count // 4):
        total = total + flip(pick(box, far ^ k, 0), 4 * k, count).astype(F32)
    return total


def grad_kernel(widths, me_ref, *refs):
    n = len(widths)
    lefts, rights = refs[:n], refs[n : 2 * n]
    outs = refs[2 * n :]
    me = me_ref[0]
    coords = (me % 2, (me // 2) % 2)
    start = 0
    for left, right, width in zip(lefts, rights, widths):
        half = width // 2
        grads = dot(left[...], right[...], ((0,), (0,))).astype(BF)
        rows = grads.shape[0] // 4
        for side in range(2):
            for low in range(2):
                block = grads[(2 * side + low) * rows : (2 * side + low + 1) * rows]
                for colour in range(2):
                    mine = (coords[0] ^ low, coords[1] ^ side)
                    first, second = (mine[1], mine[0]) if colour == 0 else mine
                    part = block[:, colour * half : (colour + 1) * half]
                    outs[colour][first, second, 0, :, start : start + half] = part
        start += half


def grad_blocks(lefts, rights, count, columns=None):
    length, widths = lefts[0].shape[0], [r.shape[1] for r in rights]
    if columns is not None:
        widths[-1] = columns[1]
    n_far = count // 4
    depth = lefts[0].shape[1] // n_far
    half = sum(widths) // 2
    shape = (2, 2, n_far, depth // 4, half)
    in_specs = [pl.BlockSpec((length, depth), lambda k, me: (0, (me[0] // 4) ^ k)) for _ in lefts]
    in_specs += [pl.BlockSpec((length, w), lambda k, me: (0, 0)) for w in widths]
    if columns is not None:
        in_specs[-1] = pl.BlockSpec((length, widths[-1]), lambda k, me: (0, me[1]))
    out_spec = pl.BlockSpec((2, 2, 1) + shape[3:], lambda k, me: (0, 0, k, 0, 0))
    me = [lax.axis_index("dp").astype(jnp.int32), lax.axis_index("seq").astype(jnp.int32)]
    return pl.pallas_call(
        functools.partial(grad_kernel, widths),
        grid_spec=pltpu.PrefetchScalarGridSpec(
            num_scalar_prefetch=1, grid=(n_far,), in_specs=in_specs, out_specs=[out_spec] * 2
        ),
        out_shape=[jax.ShapeDtypeStruct(shape, BF)] * 2,
    )(jnp.stack(me), *lefts, *rights)


def scatter_grads(lefts, rights, count, columns=None):
    widths = [r.shape[1] for r in rights]
    if columns is not None:
        widths[-1] = columns[1]
    if not boxed(count) or any(w % 256 for w in widths):
        if columns is not None:
            last = lax.dynamic_slice_in_dim(rights[-1], columns[0] * columns[1], columns[1], 1)
            rights = rights[:-1] + [last]
        return [
            lax.psum_scatter(
                dot(a, b, ((0,), (0,))), "dp", scatter_dimension=0, tiled=True
            )
            for a, b in zip(lefts, rights)
        ]
    pieces = []
    for colour, grads in enumerate(grad_blocks(lefts, rights, count, columns)):
        first, second = (2, 1) if colour == 0 else (1, 2)
        got = flip(grads[1], first, count)
        keep, send = add_low(grads[0, 0], got[0]), add_low(grads[0, 1], got[1])
        pieces.append(add_low(keep, flip(send, second, count)))
    total = jnp.concatenate([p[0] for p in pieces], axis=1).astype(F32)
    for k in range(1, count // 4):
        part = jnp.concatenate([p[k] for p in pieces], axis=1)
        total = total + flip(part, 4 * k, count).astype(F32)
    sums, start, half = [], 0, sum(widths) // 2
    for width in widths:
        step = width // 2
        sums.append(
            jnp.concatenate(
                [total[:, start : start + step], total[:, half + start : half + start + step]], axis=1
            )
        )
        start += step
    return sums


PAIR = 2 * HEAD_DIM


def window(block):
    return max(0, block - REACH // BLOCK) * BLOCK, (block + 1) * BLOCK


def distances(row_ref, col_ref, block):
    start, stop = window(block)
    shape = (stop - start, BLOCK)
    key = lax.broadcasted_iota(jnp.int32, shape, 0) + start
    query = lax.broadcasted_iota(jnp.int32, shape, 1) + block * BLOCK
    same = col_ref[start:stop, :] == row_ref[:, block * BLOCK : (block + 1) * BLOCK]
    return jnp.where((query >= key) & same, (query - key).astype(F32), FAR)


def chances_of(query, key, far, slope):
    scores = dot(key, query, ((1,), (1,))) - slope * far
    top = jnp.max(scores, axis=0, keepdims=True)
    grown = jnp.exp(scores - top)
    return grown * (1.0 / jnp.sum(grown, axis=0, keepdims=True))


def attend_kernel(n_blocks, first, slope_ref, row_ref, col_ref, qkv_ref, o_ref, *far_refs):
    pair = pl.program_id(0)

    @pl.when(pair == 0)
    def _():
        for block in range(n_blocks):
            far_refs[block][...] = distances(row_ref, col_ref, block)

    left = lax.broadcasted_iota(jnp.int32, (BLOCK, PAIR), 1) < HEAD_DIM
    for block in range(n_blocks):
        start, stop = window(block)
        rows = slice(block * BLOCK, (block + 1) * BLOCK)
        query = qkv_ref[rows, :PAIR] * BF(HEAD_DIM**-0.5)
        key, value = qkv_ref[start:stop, PAIR : 2 * PAIR], qkv_ref[start:stop, 2 * PAIR :]
        parts = []
        for side in range(2):
            mine = jnp.where(left if side == 0 else ~left, query, 0)
            slope = slope_ref[2 * (pair + first) + side]
            share = chances_of(mine, key, far_refs[block][...], slope).astype(BF)
            parts.append(dot(share, value, ((0,), (0,))))
        o_ref[rows, :] = jnp.where(left, parts[0], parts[1]).astype(BF)


def attend_back_kernel(
    n_blocks, first, slope_ref, row_ref, col_ref, qkv_ref, g_ref, d_ref, k_sum, v_sum, *far_refs
):
    pair = pl.program_id(0)

    @pl.when(pair == 0)
    def _():
        for block in range(n_blocks):
            far_refs[block][...] = distances(row_ref, col_ref, block)

    left = lax.broadcasted_iota(jnp.int32, (BLOCK, PAIR), 1) < HEAD_DIM
    scale = HEAD_DIM**-0.5
    for block in range(n_blocks):
        start, stop = window(block)
        rows = slice(block * BLOCK, (block + 1) * BLOCK)
        wide = lax.broadcasted_iota(jnp.int32, (stop - start, PAIR), 1) < HEAD_DIM
        query = qkv_ref[rows, :PAIR] * BF(scale)
        grad = g_ref[rows, :]
        key, value = qkv_ref[start:stop, PAIR : 2 * PAIR], qkv_ref[start:stop, 2 * PAIR :]
        dq, dk, dv = [], [], []
        for side in range(2):
            keep = left if side == 0 else ~left
            slope = slope_ref[2 * (pair + first) + side]
            chances = chances_of(jnp.where(keep, query, 0), key, far_refs[block][...], slope)
            g_chances = dot(value, jnp.where(keep, grad, 0), ((1,), (1,)))
            product = chances * g_chances
            inner = jnp.sum(product, axis=0, keepdims=True)
            g_scores = (product - chances * inner).astype(BF)
            dv.append(matmul(chances.astype(BF), grad))
            dk.append(matmul(g_scores, query))
            dq.append(dot(g_scores, key, ((0,), (0,))))
        d_ref[rows, :PAIR] = (jnp.where(left, dq[0], dq[1]) * scale).astype(BF)
        dk, dv = jnp.where(wide, dk[0], dk[1]), jnp.where(wide, dv[0], dv[1])
        old = block * BLOCK - start
        if old:
            k_sum[start : start + old, :] += dk[:old]
            v_sum[start : start + old, :] += dv[:old]
        k_sum[rows, :] = dk[old:]
        v_sum[rows, :] = dv[old:]
    d_ref[:, PAIR : 2 * PAIR] = k_sum[...].astype(BF)
    d_ref[:, 2 * PAIR :] = v_sum[...].astype(BF)


def far_scratch(length):
    return [
        pltpu.VMEM((window(block)[1] - window(block)[0], BLOCK), F32)
        for block in range(length // BLOCK)
    ]


def attend_specs(length, first, widths):
    fixed = [
        pl.BlockSpec(memory_space=pltpu.SMEM),
        pl.BlockSpec((1, length), lambda p: (0, 0)),
        pl.BlockSpec((length, 1), lambda p: (0, 0)),
    ]
    return fixed + [pl.BlockSpec((length, w), lambda p: (0, p + first)) for w in widths]


def attend(slopes, row, col, qkv, pairs):
    length = qkv.shape[0]
    return pl.pallas_call(
        functools.partial(attend_kernel, length // BLOCK, pairs[0]),
        out_shape=jax.ShapeDtypeStruct((length, len(pairs) * PAIR), BF),
        grid=(len(pairs),),
        in_specs=attend_specs(length, pairs[0], [3 * PAIR]),
        out_specs=pl.BlockSpec((length, PAIR), lambda p: (0, p)),
        scratch_shapes=far_scratch(length),
    )(slopes, row, col, qkv)


def attend_back(slopes, row, col, qkv, grads, pairs):
    length = qkv.shape[0]
    return pl.pallas_call(
        functools.partial(attend_back_kernel, length // BLOCK, pairs[0]),
        out_shape=jax.ShapeDtypeStruct((length, len(pairs) * 3 * PAIR), BF),
        grid=(len(pairs),),
        in_specs=attend_specs(length, pairs[0], [3 * PAIR, PAIR]),
        out_specs=pl.BlockSpec((length, 3 * PAIR), lambda p: (0, p)),
        scratch_shapes=[pltpu.VMEM((length, PAIR), F32)] * 2 + far_scratch(length),
    )(slopes, row, col, qkv, grads)


def normed(matrix):
    centred = matrix - jnp.mean(matrix, axis=-1, keepdims=True)
    spread = jnp.mean(centred * centred, axis=-1, keepdims=True)
    inverse = lax.rsqrt(spread + EPS)
    return centred * inverse, inverse


def norm_back(grad, gain, unit, inverse):
    scaled = grad * gain
    return inverse * (
        scaled
        - jnp.mean(scaled, axis=-1, keepdims=True)
        - unit * jnp.mean(scaled * unit, axis=-1, keepdims=True)
    )


def gelu_and_slope(u):
    c = 0.7978845608
    t = jnp.tanh(c * (u + 0.044715 * u * u * u))
    slope = 0.5 * (1.0 + t) + 0.5 * u * (1.0 - t * t) * (c * (1.0 + 3 * 0.044715 * u * u))
    return 0.5 * u * (1.0 + t), slope


def make_body(dp, seq):
    def body(
        tokens, segments, cotangent,
        query_weight, key_weight, value_weight, out_weight, up_weight, down_weight,
        query_bias, value_bias, out_bias, up_bias, down_bias,
        first_gain, first_shift, second_gain, second_shift,
    ):
        me_seq = lax.axis_index("seq")
        _, local, width = tokens.shape
        length = segments.shape[1]
        rows = query_weight.shape[0]
        hidden = up_weight.shape[1]
        hidden_rows = down_weight.shape[0]
        head_cols = width // seq
        heads = HEADS // seq
        hidden_cols = hidden // seq

        pairs = heads // 2
        small_params = (
            query_bias, value_bias, out_bias, up_bias, down_bias,
            first_gain, first_shift, second_gain, second_shift,
        )
        small_sizes = [v.shape[0] for v in small_params]
        offsets = [sum(small_sizes[:i]) for i in range(len(small_sizes))]

        qkv_own = jnp.stack(
            [w.reshape(rows, seq, pairs, PAIR) for w in (query_weight, key_weight, value_weight)], 3
        ).transpose(1, 0, 2, 3, 4)
        qkv_own = seq_swap(qkv_own.reshape(seq, rows, 3 * head_cols), seq)
        (qkv_full,), mark = gather_blocks([qkv_own.reshape(seq * rows, 3 * head_cols)], dp)

        small = jnp.concatenate(small_params)
        small_all = seq_gather(small, seq).reshape(-1, 128)
        small_all = gather_small(small_all, dp).reshape(dp * seq, -1)

        up_own = up_weight.reshape(rows, dp, seq, hidden_rows).transpose(2, 0, 1, 3)
        out_own = out_weight.reshape(rows, seq, head_cols).transpose(1, 0, 2)
        up_own = jnp.concatenate([up_own.reshape(seq, rows, hidden_cols), out_own], axis=2)
        up_own = seq_swap(up_own, seq).reshape(seq * rows, -1)
        (up_full, out_half), mark = gather_blocks(
            [up_own[:, :hidden_cols], up_own[:, hidden_cols:]], dp, mark
        )
        out_full = seq_columns(out_half, seq)
        (down_full,), _ = gather_blocks([down_weight], dp, mark)

        tokens_all = seq_gather(tokens[0], seq).reshape(length, width)
        grad_output = seq_gather(cotangent[0], seq).reshape(length, width)

        def small_of(index):
            return small_all[:, offsets[index] : offsets[index] + small_sizes[index]].reshape(-1)

        (q_shift, v_shift, o_shift, u_shift, d_shift, gain_one, shift_one, gain_two, shift_two) = [
            small_of(i) for i in range(9)
        ]

        def own_pairs(vector):
            return lax.dynamic_slice_in_dim(vector, me_seq * head_cols, head_cols, 0).reshape(pairs, PAIR)

        u_own = pick(u_shift.reshape(dp, seq, hidden_rows), me_seq, 1).reshape(-1)
        qkv_shift = jnp.stack(
            [own_pairs(q_shift), jnp.zeros((pairs, PAIR), F32), own_pairs(v_shift)], axis=1
        ).reshape(-1)

        inputs = tokens_all.astype(F32)
        unit_one, _ = normed(inputs)
        first_low = (unit_one * gain_one + shift_one).astype(BF)
        qkv = (matmul(first_low, qkv_full) + qkv_shift).astype(BF)
        ids = (me_seq * heads + jnp.arange(heads) + 1).astype(F32)
        slopes = 2.0 ** (-8.0 * ids / HEADS)
        row, col = segments.reshape(1, length), segments.reshape(length, 1)
        mixed_own = attend(slopes, row, col, qkv, range(pairs))
        mixed = seq_columns(mixed_own, seq)
        middle = inputs + matmul(mixed, out_full) + o_shift
        unit_two, inverse_two = normed(middle)
        second_low = (unit_two * gain_two + shift_two).astype(BF)
        hidden_pre = matmul(second_low, up_full) + u_own
        activated, hidden_slope = gelu_and_slope(hidden_pre)
        activated = activated.astype(BF)
        hidden_slope = hidden_slope.astype(BF)

        (down_sum,) = scatter_grads([activated], [grad_output], dp)
        g_hidden = (dot(grad_output, down_full, ((1,), (1,))) * hidden_slope.astype(F32)).astype(BF)
        (up_sum,) = scatter_grads([second_low], [g_hidden], dp)
        g_second = seq_total(dot(g_hidden, up_full, ((1,), (1,))), seq, BF)
        g_middle = grad_output.astype(F32) + norm_back(g_second, gain_two, unit_two, inverse_two)
        g_attn = g_middle.astype(BF)
        out_own = lax.dynamic_slice_in_dim(out_full, me_seq * head_cols, head_cols, 0)
        g_mixed = dot(g_attn, out_own, ((1,), (1,))).astype(BF)
        groups = [range(pairs // 2), range(pairs // 2, pairs)] if pairs > 1 else [range(pairs)]
        g_qkv = [attend_back(slopes, row, col, qkv, g_mixed, group) for group in groups]
        first_sum, out_sum = scatter_grads(
            [first_low, mixed], [g_qkv[0], g_attn], dp, (me_seq, head_cols)
        )
        qkv_sums = [first_sum] + [scatter_grads([first_low], [part], dp)[0] for part in g_qkv[1:]]
        g_qkv = jnp.concatenate(g_qkv, axis=1)
        g_first = dot(g_qkv, qkv_full, ((1,), (1,))).reshape(seq, local, width)
        g_first = seq_reduce(g_first, seq, BF)
        unit_own, inverse_own = normed(tokens[0].astype(F32))
        g_middle_own = pick(g_middle.reshape(seq, local, width), me_seq, 0)
        input_grad = g_middle_own + norm_back(g_first, gain_one, unit_own, inverse_own)

        lowered = matmul(activated, down_full).reshape(seq, local, width)
        middle_own = pick(middle.reshape(seq, local, width), me_seq, 0)
        output = (middle_own + seq_reduce(lowered, seq, F32) + d_shift).astype(BF)[None]

        def to_rows(total):
            return seq_swap(total.reshape(seq, rows, -1), seq).transpose(1, 0, 2)

        qkv_rows = to_rows(jnp.concatenate(qkv_sums, axis=1))
        qkv_rows = qkv_rows.reshape(rows, seq, pairs, 3, PAIR)
        weight_grads = [qkv_rows[:, :, :, i].reshape(rows, width) for i in range(3)]
        up_rows = to_rows(jnp.concatenate([up_sum, out_sum], axis=1))
        up_grad = (
            up_rows[:, :, :hidden_cols]
            .reshape(rows, seq, dp, hidden_rows)
            .transpose(0, 2, 1, 3)
            .reshape(rows, hidden)
        )
        out_grad = up_rows[:, :, hidden_cols:].reshape(rows, width)

        def sums(matrix):
            return jnp.sum(matrix.astype(F32), axis=0)

        mine = jnp.arange(seq) == me_seq

        def heads_only(vector):
            return jnp.where(mine[:, None], vector.reshape(1, -1), 0.0).reshape(-1)

        share = 1.0 / seq
        qkv_columns = sums(g_qkv).reshape(pairs, 3, PAIR)
        up_bias_grad = jnp.where(
            mine[None, :, None], sums(g_hidden).reshape(dp, 1, hidden_rows), 0.0
        )
        vectors = [
            heads_only(qkv_columns[:, 0]), heads_only(qkv_columns[:, 2]), sums(g_attn) * share,
            up_bias_grad, sums(cotangent[0]), sums(g_first * unit_own), sums(g_first),
            sums(g_second * unit_two) * share, sums(g_second) * share,
        ]
        packed = jnp.concatenate(
            [v.reshape(dp, seq, m) for v, m in zip(vectors, small_sizes)], axis=2
        ).reshape(dp, seq * sum(small_sizes) // 128, 128)
        if boxed(dp):
            small_sum = scatter_far(scatter_near(packed, dp, 0), dp)
        else:
            small_sum = lax.psum_scatter(packed, "dp", scatter_dimension=0, tiled=False)
        small_grad = seq_reduce(small_sum.reshape(seq, -1), seq, F32)
        small_grads = [
            small_grad[offsets[i] : offsets[i] + small_sizes[i]] for i in range(9)
        ]
        return (
            output, input_grad[None], *weight_grads, out_grad, up_grad, down_sum, *small_grads
        )

    return body


def solution(mesh):
    both = ("dp", "seq")
    matrix, vector = P(both, None), P(both)
    dp, seq = mesh.shape["dp"], mesh.shape["seq"]
    layer = make_body(dp, seq)

    return jax.shard_map(
        layer,
        mesh=mesh,
        in_specs=(P("dp", "seq", None), P("dp", None), P("dp", "seq", None))
        + (matrix,) * 6
        + (vector,) * 9,
        out_specs=(P("dp", "seq", None),) * 2 + (matrix,) * 6 + (vector,) * 9,
        check_vma=False,
    )
```

```python
import functools

import jax
import jax.numpy as jnp
from jax import lax
from jax.experimental import pallas as pl
from jax.experimental.pallas import tpu as pltpu
from jax.sharding import PartitionSpec as P


HEADS = 16
HEAD_DIM = 64
EPS = 1e-05
FAR = 1e30
BLOCK = 256
REACH = 512
BF = jnp.bfloat16
F32 = jnp.float32


def dot(left, right, contract):
    return lax.dot_general(left, right, (contract, ((), ())), preferred_element_type=F32)


def matmul(left, right):
    return dot(left, right, ((1,), (0,)))


def pick(array, index, axis):
    return lax.dynamic_index_in_dim(array, index, axis, keepdims=False)


def trade(array):
    return lax.ppermute(array, "seq", [(0, 1), (1, 0)])


def seq_gather(block, seq):
    if seq == 2:
        other = trade(block)
        first = lax.axis_index("seq") == 0
        return jnp.where(first, jnp.stack([block, other]), jnp.stack([other, block]))
    return lax.all_gather(block, "seq", axis=0)


def seq_swap(blocks, seq):
    if seq == 2:
        me = lax.axis_index("seq")
        own, other = pick(blocks, me, 0), trade(pick(blocks, 1 - me, 0))
        return jnp.where(me == 0, jnp.stack([own, other]), jnp.stack([other, own]))
    return lax.all_to_all(blocks, "seq", 0, 0)


def seq_reduce(blocks, seq, send):
    if seq == 2:
        me = lax.axis_index("seq")
        other = trade(pick(blocks, 1 - me, 0).astype(send))
        return pick(blocks, me, 0).astype(F32) + other.astype(F32)
    return lax.psum_scatter(blocks.astype(F32), "seq", scatter_dimension=0, tiled=False)


def flip(array, bits, count):
    return lax.ppermute(array, "dp", [(i, i ^ bits) for i in range(count)])


def boxed(count):
    return count >= 4 and not count & (count - 1)


def vmem_specs(count):
    return [pl.BlockSpec(memory_space=pltpu.VMEM)] * count


def split_kernel(me_ref, *refs):
    weights, up_ref, targets = refs[:4], refs[4], refs[5:]
    me, cols = me_ref[0], targets[0].shape[1] // 4
    tile = PAIR
    for away in range(2):
        first_ref, up_out = targets[away], targets[2 + away]
        base, start = (me ^ away) * cols, 0
        for colour in range(2):
            for at in range(colour * cols // 2, (colour + 1) * cols // 2, PAIR):
                for weight in weights[:3]:
                    column = pl.multiple_of(base + at, PAIR)
                    first_ref[:, start : start + PAIR] = weight[:, pl.ds(column, PAIR)]
                    start += PAIR
            column = pl.multiple_of(base + colour * (cols // 2), cols // 2)
            first_ref[:, start : start + cols // 2] = weights[3][:, pl.ds(column, cols // 2)]
            start += cols // 2
        for at in range(0, up_out.shape[1], tile):
            column = pl.multiple_of(2 * at + (me ^ away) * tile, tile)
            up_out[:, at : at + tile] = up_ref[:, pl.ds(column, tile)]


def split_weights(me, weights, up_weight):
    rows, width = weights[0].shape
    shapes = [(rows, 2 * width)] * 2 + [(rows, up_weight.shape[1] // 2)] * 2
    return pl.pallas_call(
        split_kernel,
        in_specs=[pl.BlockSpec(memory_space=pltpu.SMEM)] + vmem_specs(5),
        out_specs=vmem_specs(4),
        out_shape=[jax.ShapeDtypeStruct(shape, BF) for shape in shapes],
    )(me.astype(jnp.int32)[None], *weights, up_weight)


def two_rows(own, other, me):
    return jnp.where(
        me == 0, jnp.concatenate([own, other], axis=0), jnp.concatenate([other, own], axis=0)
    )


def pack_kernel(*refs):
    slots, outs = refs[:-2], refs[-2:]
    half = outs[0].shape[2]
    for k, slot in enumerate(slots):
        for colour in range(2):
            outs[colour][k] = slot[:, colour * half : (colour + 1) * half]


def put_pieces(me, pieces, targets):
    low, side, far = me % 2, (me // 2) % 2, me // 4
    n_far, rows, _ = pieces[0].shape
    for colour in range(2):
        for late in range(2):
            for early in range(2):
                piece = pieces[4 * colour + 2 * late + early]
                away = (early, late) if colour == 0 else (late, early)
                for k in range(n_far):
                    block = (far ^ k) * 4 + (side ^ away[1]) * 2 + (low ^ away[0])
                    at = pl.multiple_of(block * rows, rows)
                    start = 0
                    for ref, column, width in targets:
                        half = width // 2
                        first = column + colour * half
                        ref[pl.ds(at, rows), first : first + half] = piece[k, :, start : start + half]
                        start += half


def whole_spec(array):
    return pl.BlockSpec(array.shape, lambda i, *_: (0,) * array.ndim)


def gather_blocks(block, widths, count, after=None):
    rows, half = block.shape[0], block.shape[1] // 2
    if not boxed(count) or any(w % 256 for w in widths):
        whole = lax.all_gather(block, "dp", axis=0, tiled=True)
        starts = [sum(widths[:i]) // 2 for i in range(len(widths))]
        return [
            jnp.concatenate(
                [whole[:, at : at + w // 2], whole[:, half + at : half + at + w // 2]], axis=1
            )
            for at, w in zip(starts, widths)
        ], block
    n_far = count // 4
    if after is not None:
        block, _ = lax.optimization_barrier((block, after))
    slots = [block] + [flip(block, 4 * k, count) for k in range(1, n_far)]
    fars = pl.pallas_call(
        pack_kernel,
        in_specs=vmem_specs(n_far),
        out_specs=vmem_specs(2),
        out_shape=[jax.ShapeDtypeStruct((n_far, rows, half), block.dtype)] * 2,
    )(*slots)
    pieces = []
    for colour, far in enumerate(fars):
        first, second = (1, 2) if colour == 0 else (2, 1)
        got = flip(far, first, count)
        pieces += [far, got, flip(far, second, count)]
        pieces += [flip(got, second, count)]
    return pieces, slots[-1]


def gather_small(block, count):
    if not boxed(count):
        return lax.all_gather(block, "dp", axis=0)
    near = jnp.stack([block, flip(block, 1, count)])
    near = jnp.stack([near, flip(near, 2, count)])
    whole = jnp.stack([near] + [flip(near, 4 * k, count) for k in range(1, count // 4)]).reshape((count,) + block.shape)
    ids = jnp.arange(count)
    order = ((ids[:, None] ^ lax.axis_index("dp")) == ids[None, :]).astype(F32)
    return jnp.sum(order.reshape(count, count, 1, 1) * whole[None], axis=1)


def add_low(a, b):
    return (a.astype(F32) + b.astype(F32)).astype(b.dtype)


def scatter_near(grads, count, colour):
    me = lax.axis_index("dp")
    side, low = (me // 2) % 2, me % 2
    box = grads.reshape((count // 4, 2, 2) + grads.shape[1:])
    if colour == 0:
        order = ((1, 2, side), (1, 1, low))
    else:
        order = ((2, 1, low), (1, 2, side))
    for axis, bit, mine in order:
        got = flip(pick(box, 1 - mine, axis), bit, count)
        box = add_low(pick(box, mine, axis), got)
    return box


def scatter_far(box, count):
    far = lax.axis_index("dp") // 4
    total = pick(box, far, 0).astype(F32)
    for k in range(1, count // 4):
        total = total + flip(pick(box, far ^ k, 0), 4 * k, count).astype(F32)
    return total


def grad_kernel(widths, ways, me_ref, *refs):
    n = len(widths)
    lefts, rights, outs, scratch = refs[:n], refs[n : 2 * n], refs[2 * n : -1], refs[-1]
    low, side = me_ref[0] % 2, (me_ref[0] // 2) % 2
    rows, start = scratch.shape[1] // 4, 0
    for left, right, width in zip(lefts, rights, widths):
        for away in range(2):
            at = pl.multiple_of((side ^ away) * 2 * rows, 2 * rows)
            if rows % 128:
                part = left[:, pl.ds(at, 2 * rows)]
                turned = jnp.concatenate([part[:, rows:], part[:, :rows]], axis=1)
                scratch[:, 2 * away * rows : 2 * (away + 1) * rows] = jnp.where(low == 0, part, turned)
            else:
                for step in range(2):
                    at_low = pl.multiple_of(at + (low ^ step) * rows, rows)
                    scratch[:, (2 * away + step) * rows : (2 * away + step + 1) * rows] = left[
                        :, pl.ds(at_low, rows)
                    ]
        grads = dot(scratch[...], right[...], ((0,), (0,)))
        for side_away in range(2):
            for low_away in range(2):
                at = (2 * side_away + low_away) * rows
                for way, (colour, low_column, high_column) in enumerate(ways):
                    first, second = (side_away, low_away) if colour == 0 else (low_away, side_away)
                    lo, hi = max(start, low_column), min(start + width, high_column)
                    outs[2 * way + first][second, 0, :, lo - low_column : hi - low_column] = grads[
                        at : at + rows, lo - start : hi - start
                    ].astype(BF)
        start += width


def grad_blocks(lefts, rights, widths, column, count, ways):
    length, n_far = lefts[0].shape[0], count // 4
    depth = lefts[0].shape[1] // n_far
    shapes = [(2, n_far, depth // 4, high - low) for _, low, high in ways for _ in range(2)]
    in_specs = [pl.BlockSpec((length, depth), lambda k, me: (0, (me[0] // 4) ^ k)) for _ in lefts]
    in_specs += [pl.BlockSpec((length, w), lambda k, me: (0, 0)) for w in widths]
    if column:
        in_specs[-1] = pl.BlockSpec((length, widths[-1]), lambda k, me: (0, me[1]))
    me = [lax.axis_index("dp").astype(jnp.int32), lax.axis_index("seq").astype(jnp.int32)]
    return pl.pallas_call(
        functools.partial(grad_kernel, widths, ways),
        grid_spec=pltpu.PrefetchScalarGridSpec(
            num_scalar_prefetch=1,
            grid=(n_far,),
            in_specs=in_specs,
            out_specs=[
                pl.BlockSpec((2, 1) + shape[2:], lambda k, me: (0, k, 0, 0)) for shape in shapes
            ],
            scratch_shapes=[pltpu.VMEM((length, depth), BF)],
        ),
        out_shape=[jax.ShapeDtypeStruct(shape, BF) for shape in shapes],
    )(jnp.stack(me), *lefts, *rights)


def scatter_grads(lefts, rights, count, colours, column=0):
    widths = [r.shape[1] for r in rights]
    if column:
        widths[-1] = column
    if not boxed(count) or any(w % 128 for w in widths) or any(a.shape[1] % (64 * count) for a in lefts):
        if column:
            last = lax.dynamic_slice_in_dim(
                rights[-1], lax.axis_index("seq") * column, column, 1
            )
            rights = rights[:-1] + [last]
        return [
            lax.psum_scatter(dot(a, b, ((0,), (0,))), "dp", scatter_dimension=0, tiled=True)
            for a, b in zip(lefts, rights)
        ]
    step = sum(widths) // len(colours)
    ways = [(colour, i * step, (i + 1) * step) for i, colour in enumerate(colours)]
    grads = grad_blocks(lefts, rights, widths, column, count, ways)
    ends = []
    for way, colour in enumerate(colours):
        keep, give = grads[2 * way : 2 * way + 2]
        first, second = (2, 1) if colour == 0 else (1, 2)
        got = flip(give, first, count)
        late = flip(add_low(keep[1], got[1]), second, count)
        ends.append((add_low(keep[0], got[0]), late))
    total = jnp.concatenate([k[0].astype(F32) + l[0].astype(F32) for k, l in ends], axis=1)
    for k in range(1, count // 4):
        part = jnp.concatenate([add_low(keep[k], late[k]) for keep, late in ends], axis=1)
        total = total + flip(part, 4 * k, count).astype(F32)
    sums, start = [], 0
    for width in widths:
        sums.append(total[:, start : start + width])
        start += width
    return sums


PAIR = 2 * HEAD_DIM


def window(block):
    return max(0, block - REACH // BLOCK) * BLOCK, (block + 1) * BLOCK


def distances(row_ref, col_ref, block, out_ref):
    start, stop = window(block)
    shape = (stop - start, BLOCK)
    key = lax.broadcasted_iota(jnp.int32, shape, 0) + start
    query = lax.broadcasted_iota(jnp.int32, shape, 1) + block * BLOCK
    same = col_ref[start:stop, :] == row_ref[:, block * BLOCK : (block + 1) * BLOCK]
    out_ref[...] = jnp.where((query >= key) & same, (query - key).astype(F32), FAR)


def all_distances(row_ref, col_ref, n_blocks, near_refs, far_ref):
    @pl.when(pl.program_id(0) == 0)
    def _():
        for block in range(n_blocks):
            wide = block - REACH // BLOCK
            target = far_ref.at[wide] if wide >= 0 else near_refs[block]
            distances(row_ref, col_ref, block, target)


def each_block(n_blocks, near_refs, far_ref, work):
    back = REACH // BLOCK
    for block in range(back):
        start, stop = window(block)
        work(block * BLOCK, start, stop - start, near_refs[block])

    for block in range(back, n_blocks):
        work(block * BLOCK, block * BLOCK - REACH, REACH + BLOCK, far_ref.at[block - back])


def chances_of(query, key, far, slope):
    scores = dot(key, query, ((1,), (1,))) - slope * far
    top = jnp.max(scores, axis=0, keepdims=True)
    grown = jnp.exp(scores - top)
    return grown * (1.0 / jnp.sum(grown, axis=0, keepdims=True))


def attend_kernel(n_blocks, first_ref, slope_ref, row_ref, col_ref, qkv_ref, o_ref, far_ref, *near_refs):
    pair = pl.program_id(0) + first_ref[0]
    all_distances(row_ref, col_ref, n_blocks, near_refs, far_ref)
    left = lax.broadcasted_iota(jnp.int32, (BLOCK, PAIR), 1) < HEAD_DIM

    def work(at, start, keys, distance_ref):
        rows, cols = pl.ds(at, BLOCK), pl.ds(start, keys)
        query = qkv_ref[rows, :PAIR] * BF(HEAD_DIM**-0.5)
        key, value = qkv_ref[cols, PAIR : 2 * PAIR], qkv_ref[cols, 2 * PAIR :]
        parts = []
        for side in range(2):
            mine = jnp.where(left if side == 0 else ~left, query, 0)
            share = chances_of(mine, key, distance_ref[...], slope_ref[2 * pair + side]).astype(BF)
            parts.append(dot(share, value, ((0,), (0,))))
        o_ref[rows, :] = jnp.where(left, parts[0], parts[1]).astype(BF)

    each_block(n_blocks, near_refs, far_ref, work)


def attend_back_kernel(
    n_blocks, first_ref, slope_ref, row_ref, col_ref, qkv_ref, g_ref, d_ref, k_sum, v_sum, far_ref, *near_refs
):
    pair = pl.program_id(0) + first_ref[0]
    all_distances(row_ref, col_ref, n_blocks, near_refs, far_ref)
    left = lax.broadcasted_iota(jnp.int32, (BLOCK, PAIR), 1) < HEAD_DIM
    scale = HEAD_DIM**-0.5

    def work(at, start, keys, distance_ref):
        rows, cols = pl.ds(at, BLOCK), pl.ds(start, keys)
        wide = lax.broadcasted_iota(jnp.int32, (keys, PAIR), 1) < HEAD_DIM
        query = qkv_ref[rows, :PAIR] * BF(scale)
        grad = g_ref[rows, :]
        key, value = qkv_ref[cols, PAIR : 2 * PAIR], qkv_ref[cols, 2 * PAIR :]
        dq, dk, dv = [], [], []
        for side in range(2):
            keep = left if side == 0 else ~left
            chances = chances_of(
                jnp.where(keep, query, 0), key, distance_ref[...], slope_ref[2 * pair + side]
            )
            g_chances = dot(value, jnp.where(keep, grad, 0), ((1,), (1,)))
            product = chances * g_chances
            inner = jnp.sum(product, axis=0, keepdims=True)
            g_scores = (product - chances * inner).astype(BF)
            dv.append(matmul(chances.astype(BF), grad))
            dk.append(matmul(g_scores, query))
            dq.append(dot(g_scores, key, ((0,), (0,))))
        d_ref[rows, :PAIR] = (jnp.where(left, dq[0], dq[1]) * scale).astype(BF)
        dk, dv = jnp.where(wide, dk[0], dk[1]), jnp.where(wide, dv[0], dv[1])
        old = keys - BLOCK
        if old:
            k_sum[pl.ds(start, old), :] += dk[:old]
            v_sum[pl.ds(start, old), :] += dv[:old]
        k_sum[rows, :] = dk[old:]
        v_sum[rows, :] = dv[old:]

    each_block(n_blocks, near_refs, far_ref, work)
    d_ref[:, PAIR : 2 * PAIR] = k_sum[...].astype(BF)
    d_ref[:, 2 * PAIR :] = v_sum[...].astype(BF)


def distance_scratch(length):
    back = REACH // BLOCK
    near = [pltpu.VMEM((window(block)[1] - window(block)[0], BLOCK), F32) for block in range(back)]
    return [pltpu.VMEM((length // BLOCK - back, REACH + BLOCK, BLOCK), F32)] + near


def attend_call(kernel, slopes, row, col, arrays, widths, out_width, sums, pairs):
    length = row.shape[1]
    in_specs = [
        pl.BlockSpec(memory_space=pltpu.SMEM),
        pl.BlockSpec((1, length), lambda p, first: (0, 0)),
        pl.BlockSpec((length, 1), lambda p, first: (0, 0)),
    ] + [pl.BlockSpec((length, w), lambda p, first: (0, p + first[0])) for w in widths]
    return pl.pallas_call(
        functools.partial(kernel, length // BLOCK),
        grid_spec=pltpu.PrefetchScalarGridSpec(
            num_scalar_prefetch=1,
            grid=(len(pairs),),
            in_specs=in_specs,
            out_specs=pl.BlockSpec((length, out_width), lambda p, first: (0, p)),
            scratch_shapes=[pltpu.VMEM((length, PAIR), F32)] * sums + distance_scratch(length),
        ),
        out_shape=jax.ShapeDtypeStruct((length, len(pairs) * out_width), BF),
    )(jnp.full((1,), pairs[0], jnp.int32), slopes, row, col, *arrays)


def attend(slopes, row, col, qkv, pairs):
    return attend_call(attend_kernel, slopes, row, col, [qkv], [3 * PAIR], PAIR, 0, pairs)


def attend_back(slopes, row, col, qkv, grads, pairs):
    return attend_call(attend_back_kernel, slopes, row, col, [qkv, grads], [3 * PAIR, PAIR], 3 * PAIR, 2, pairs)


def normed(matrix):
    centred = matrix - jnp.mean(matrix, axis=-1, keepdims=True)
    spread = jnp.mean(centred * centred, axis=-1, keepdims=True)
    inverse = lax.rsqrt(spread + EPS)
    return centred * inverse, inverse


def norm_back(grad, gain, unit, inverse):
    scaled = grad * gain
    return inverse * (
        scaled
        - jnp.mean(scaled, axis=-1, keepdims=True)
        - unit * jnp.mean(scaled * unit, axis=-1, keepdims=True)
    )


def gelu_and_slope(u):
    c = 0.7978845608
    square = u * u
    t = jnp.tanh(u * (c + (c * 0.044715) * square))
    half = 0.5 + 0.5 * t
    slope = half + (u - u * (t * t)) * (0.5 * c + (1.5 * c * 0.044715) * square)
    return u * half, slope


ROWS = 256
COLS = 512


def middle_kernel(n, me_ref, *refs):
    mixed_parts, weights = refs[:n], refs[n : 2 * n]
    x_ref, shift_ref, gain_ref, bias_ref, mixed_ref, middle_ref, low_ref = refs[2 * n :]
    for i in range(n):
        width = mixed_parts[i].shape[1]
        at = pl.multiple_of(me_ref[1 + i] * width, width)
        mixed_ref[:, pl.ds(at, width)] = mixed_parts[i][...]
    mixed = mixed_ref[...]
    for i in range(n):
        width = weights[i].shape[1]
        at = pl.multiple_of(me_ref[1 + i] * width, width)
        middle_ref[:, pl.ds(at, width)] = matmul(mixed, weights[i][...])
    middle = x_ref[...].astype(F32) + middle_ref[...] + shift_ref[...]
    middle_ref[...] = middle
    unit, _ = normed(middle)
    low_ref[...] = (unit * gain_ref[...] + bias_ref[...]).astype(BF)


def middle_of(me, mixed_parts, weights, inputs, shift, gain, bias):
    n, (length, width) = len(weights), inputs.shape
    rows = lambda w: pl.BlockSpec((ROWS, w), lambda i, me: (i, 0))
    whole = lambda r, w: pl.BlockSpec((r, w), lambda i, me: (0, 0))
    return pl.pallas_call(
        functools.partial(middle_kernel, n),
        grid_spec=pltpu.PrefetchScalarGridSpec(
            num_scalar_prefetch=1,
            grid=(length // ROWS,),
            in_specs=[rows(p.shape[1]) for p in mixed_parts]
            + [whole(*w.shape) for w in weights]
            + [rows(width)]
            + [whole(1, width)] * 3,
            out_specs=[rows(width)] * 3,
        ),
        out_shape=[jax.ShapeDtypeStruct((length, width), t) for t in (BF, F32, BF)],
    )(me, *mixed_parts, *weights, inputs, shift[None], gain[None], bias[None])


def qkv_kernel(me_ref, *refs):
    pieces, (low_ref, bias_ref, qkv_ref, full_ref, out_ref, scratch) = refs[:8], refs[8:]
    step = pl.program_id(0)
    width = scratch.shape[1]

    @pl.when(step == 0)
    def _():
        put_pieces(me_ref[0], pieces, [(scratch, 0, width), (out_ref, 0, out_ref.shape[1])])

    cols = qkv_ref.shape[1]
    weight = scratch[:, pl.ds(pl.multiple_of(step * cols, cols), cols)]
    full_ref[...] = weight
    qkv_ref[...] = (matmul(low_ref[...], weight) + bias_ref[...]).astype(BF)


def qkv_of(me, pieces, first_low, bias, head_cols):
    if len(pieces) == 2:
        return (matmul(first_low, pieces[0]) + bias).astype(BF), *pieces
    length, width = first_low.shape
    cols = pl.BlockSpec((length, head_cols), lambda i, me: (0, i))
    full = pl.BlockSpec((width, head_cols), lambda i, me: (0, i))
    return pl.pallas_call(
        qkv_kernel,
        grid_spec=pltpu.PrefetchScalarGridSpec(
            num_scalar_prefetch=1,
            grid=(3,),
            in_specs=[whole_spec(p) for p in pieces]
            + [whole_spec(first_low), pl.BlockSpec((1, head_cols), lambda i, me: (0, i))],
            out_specs=[cols, full, pl.BlockSpec((width, head_cols), lambda i, me: (0, 0))],
            scratch_shapes=[pltpu.VMEM((width, 3 * head_cols), BF)],
        ),
        out_shape=[
            jax.ShapeDtypeStruct((length, 3 * head_cols), BF),
            jax.ShapeDtypeStruct((width, 3 * head_cols), BF),
            jax.ShapeDtypeStruct((width, head_cols), BF),
        ],
    )(me, *pieces, first_low, bias[None])


def up_kernel(me_ref, *refs):
    pieces, (low_ref, bias_ref, act_ref, slope_ref, full_ref, scratch) = refs[:8], refs[8:]
    step = pl.program_id(0)

    @pl.when(step == 0)
    def _():
        put_pieces(me_ref[0], pieces, [(scratch, 0, scratch.shape[1])])

    cols = act_ref.shape[1]
    weight = scratch[:, pl.ds(pl.multiple_of(step * cols, cols), cols)]
    full_ref[...] = weight
    for at in range(0, act_ref.shape[0], ROWS):
        rows = slice(at, at + ROWS)
        act, slope = gelu_and_slope(matmul(low_ref[rows, :], weight) + bias_ref[...])
        act_ref[rows, :] = act.astype(BF)
        slope_ref[rows, :] = slope.astype(BF)


def up_of(me, pieces, second_low, bias):
    if len(pieces) == 1:
        act, slope = gelu_and_slope(matmul(second_low, pieces[0]) + bias)
        return act.astype(BF), slope.astype(BF), pieces[0]
    length, width = second_low.shape
    hidden = bias.shape[0]
    cols = pl.BlockSpec((length, COLS), lambda i, me: (0, i))
    return pl.pallas_call(
        up_kernel,
        grid_spec=pltpu.PrefetchScalarGridSpec(
            num_scalar_prefetch=1,
            grid=(hidden // COLS,),
            in_specs=[whole_spec(p) for p in pieces]
            + [whole_spec(second_low), pl.BlockSpec((1, COLS), lambda i, me: (0, i))],
            out_specs=[cols, cols, pl.BlockSpec((width, COLS), lambda i, me: (0, i))],
            scratch_shapes=[pltpu.VMEM((width, hidden), BF)],
        ),
        out_shape=[
            jax.ShapeDtypeStruct((length, hidden), BF),
            jax.ShapeDtypeStruct((length, hidden), BF),
            jax.ShapeDtypeStruct((width, hidden), BF),
        ],
    )(me, *pieces, second_low, bias[None])


def back_kernel(n_steps, me_ref, *refs):
    pieces, refs = refs[:8], refs[8:]
    dy_ref, slope_ref, up_ref, hidden_ref, sum_ref, full_ref, z_ref, scratch, held = refs
    step = pl.program_id(0)

    @pl.when(step == 0)
    def _():
        put_pieces(me_ref[0], pieces, [(scratch, 0, scratch.shape[1])])

    cols = hidden_ref.shape[1]

    @pl.when(step < n_steps)
    def _():
        at = pl.multiple_of(step * cols, cols)
        weight = scratch[pl.ds(at, cols), :]
        full_ref[...] = weight
        total = None
        for start in range(0, dy_ref.shape[0], ROWS):
            rows = slice(start, start + ROWS)
            g_act = dot(dy_ref[rows, :], weight, ((1,), (1,)))
            g_hidden = (g_act * slope_ref[rows, :].astype(F32)).astype(BF)
            hidden_ref[rows, :] = g_hidden
            held[rows, pl.ds(at, cols)] = g_hidden
            part = jnp.sum(g_hidden.astype(F32), axis=0, keepdims=True)
            total = part if total is None else total + part
        sum_ref[...] = total

    @pl.when(step >= n_steps)
    def _():
        z_ref[...] = dot(held[...], up_ref[...], ((1,), (1,))).astype(BF)


def back_of(me, pieces, grad_output, slope, up_full):
    length, width = grad_output.shape
    hidden = slope.shape[1]
    if len(pieces) == 1:
        g_hidden = (dot(grad_output, pieces[0], ((1,), (1,))) * slope.astype(F32)).astype(BF)
        z = dot(g_hidden, up_full, ((1,), (1,))).astype(BF)
        return g_hidden, jnp.sum(g_hidden.astype(F32), axis=0), pieces[0], z
    n_steps, n_late = hidden // COLS, width // ROWS
    early = lambda i: jnp.minimum(i, n_steps - 1)
    late = lambda i: jnp.maximum(i - n_steps, 0)
    cols = pl.BlockSpec((length, COLS), lambda i, me: (0, early(i)))
    return pl.pallas_call(
        functools.partial(back_kernel, n_steps),
        grid_spec=pltpu.PrefetchScalarGridSpec(
            num_scalar_prefetch=1,
            grid=(n_steps + n_late,),
            in_specs=[whole_spec(p) for p in pieces]
            + [whole_spec(grad_output), cols]
            + [pl.BlockSpec((ROWS, hidden), lambda i, me: (late(i), 0))],
            out_specs=[
                cols,
                pl.BlockSpec((1, COLS), lambda i, me: (0, early(i))),
                pl.BlockSpec((COLS, width), lambda i, me: (early(i), 0)),
                pl.BlockSpec((length, ROWS), lambda i, me: (0, late(i))),
            ],
            scratch_shapes=[pltpu.VMEM((hidden, width), BF), pltpu.VMEM((length, hidden), BF)],
        ),
        out_shape=[
            jax.ShapeDtypeStruct((length, hidden), BF),
            jax.ShapeDtypeStruct((1, hidden), F32),
            jax.ShapeDtypeStruct((hidden, width), BF),
            jax.ShapeDtypeStruct((length, width), BF),
        ],
    )(me, *pieces, grad_output, slope, up_full)


def turn_kernel(n, me_ref, *refs):
    own_ref, other_ref, middle_ref, dy_ref, gain_ref = refs[:5]
    weights = refs[5 : 5 + n]
    g_middle_ref, g_attn_ref, g_mixed_ref, sum_ref = refs[5 + n :]
    grad = own_ref[...].astype(F32) + other_ref[...].astype(F32)
    unit, inverse = normed(middle_ref[...])
    g_middle = dy_ref[...].astype(F32) + norm_back(grad, gain_ref[...], unit, inverse)
    g_middle_ref[...] = g_middle
    g_attn = g_middle.astype(BF)
    g_attn_ref[...] = g_attn
    total = None
    for i in range(n):
        width = weights[i].shape[1]
        at = pl.multiple_of(me_ref[1 + i] * width, width)
        part = dot(g_attn_ref[:, pl.ds(at, width)], weights[i][...], ((1,), (1,)))
        total = part if total is None else total + part
    g_mixed_ref[...] = total.astype(BF)
    sums = jnp.concatenate(
        [
            jnp.sum(v, axis=0, keepdims=True)
            for v in (grad * unit, grad, g_attn.astype(F32))
        ]
        + [jnp.zeros((5, grad.shape[1]), F32)],
        axis=0,
    )

    @pl.when(pl.program_id(0) == 0)
    def _():
        sum_ref[...] = sums

    @pl.when(pl.program_id(0) > 0)
    def _():
        sum_ref[...] += sums


def turn_of(me, own, other, middle, grad_output, gain, weights, head_cols):
    n, (length, width) = len(weights), middle.shape
    rows = lambda w: pl.BlockSpec((ROWS, w), lambda i, me: (i, 0))
    return pl.pallas_call(
        functools.partial(turn_kernel, n),
        grid_spec=pltpu.PrefetchScalarGridSpec(
            num_scalar_prefetch=1,
            grid=(length // ROWS,),
            in_specs=[rows(width)] * 4
            + [pl.BlockSpec((1, width), lambda i, me: (0, 0))]
            + [pl.BlockSpec((head_cols, w.shape[1]), lambda i, me: (me[0], 0)) for w in weights],
            out_specs=[rows(width), rows(width), rows(head_cols)]
            + [pl.BlockSpec((8, width), lambda i, me: (0, 0))],
        ),
        out_shape=[
            jax.ShapeDtypeStruct((length, width), F32),
            jax.ShapeDtypeStruct((length, width), BF),
            jax.ShapeDtypeStruct((length, head_cols), BF),
            jax.ShapeDtypeStruct((8, width), F32),
        ],
    )(me, own, other, middle, grad_output, gain[None], *weights)


def make_body(dp, seq):
    def body(
        tokens, segments, cotangent,
        query_weight, key_weight, value_weight, out_weight, up_weight, down_weight,
        query_bias, value_bias, out_bias, up_bias, down_bias,
        first_gain, first_shift, second_gain, second_shift,
    ):
        me_seq = lax.axis_index("seq")
        _, local, width = tokens.shape
        length = segments.shape[1]
        rows = query_weight.shape[0]
        hidden = up_weight.shape[1]
        hidden_rows = down_weight.shape[0]
        head_cols = width // seq
        heads = HEADS // seq
        hidden_cols = hidden // seq

        pairs = heads // 2
        small_params = (
            query_bias, value_bias, out_bias, up_bias, down_bias,
            first_gain, first_shift, second_gain, second_shift,
        )
        small_sizes = [v.shape[0] for v in small_params]
        offsets = [sum(small_sizes[:i]) for i in range(len(small_sizes))]

        def first_columns(s, colour):
            at, half = s * head_cols, head_cols // 2
            span = [pairs * colour // 2, pairs * (colour + 1) // 2] if pairs > 1 else [0, 1]
            parts = [
                w[:, at + p * PAIR : at + (p + 1) * PAIR]
                for p in range(*span)
                for w in (query_weight, key_weight, value_weight)
            ]
            if pairs == 1:
                joined = jnp.concatenate(parts, axis=1)
                parts = [joined[:, colour * 3 * half : (colour + 1) * 3 * half]]
            return parts + [out_weight[:, at + colour * half : at + (colour + 1) * half]]

        quick = seq == 2 and hidden_rows == PAIR and pairs > 1
        if quick:
            own, send, up_mine, up_send = split_weights(
                me_seq, (query_weight, key_weight, value_weight, out_weight), up_weight
            )
            first_own = two_rows(own, trade(send), me_seq)
        else:
            first_own = jnp.stack(
                [jnp.concatenate(first_columns(i, 0) + first_columns(i, 1), axis=1) for i in range(seq)]
            )
            first_own = seq_swap(first_own, seq).reshape(seq * rows, -1)
        q_pieces, mark = gather_blocks(first_own, [3 * head_cols, head_cols], dp)

        total = sum(small_sizes)
        small = sum(
            jnp.pad(v.astype(F32), (at, total - at - size))
            for v, at, size in zip(small_params, offsets, small_sizes)
        )
        small_all = seq_gather(small, seq).reshape(-1, 128)
        small_all = gather_small(small_all, dp).reshape(dp * seq, -1)

        if quick:
            up_own = two_rows(up_mine, trade(up_send), me_seq)
        else:
            up_own = up_weight.reshape(rows, dp, seq, hidden_rows).transpose(2, 0, 1, 3)
            up_own = seq_swap(up_own.reshape(seq, rows, hidden_cols), seq).reshape(seq * rows, -1)
        up_pieces, mark = gather_blocks(up_own, [hidden_cols], dp, mark)
        down_pieces, _ = gather_blocks(down_weight, [width], dp, mark)
        tokens_all = seq_gather(tokens[0], seq).reshape(length, width)
        grad_output = seq_gather(cotangent[0], seq).reshape(length, width)

        def small_of(index):
            return small_all[:, offsets[index] : offsets[index] + small_sizes[index]].reshape(-1)

        (q_shift, v_shift, o_shift, u_shift, d_shift, gain_one, shift_one, gain_two, shift_two) = [
            small_of(i) for i in range(9)
        ]

        def own_pairs(vector):
            return lax.dynamic_slice_in_dim(vector, me_seq * head_cols, head_cols, 0).reshape(pairs, PAIR)

        u_own = pick(u_shift.reshape(dp, seq, hidden_rows), me_seq, 1).reshape(-1)
        qkv_shift = jnp.stack(
            [own_pairs(q_shift), jnp.zeros((pairs, PAIR), F32), own_pairs(v_shift)], axis=1
        ).reshape(-1)

        inputs = tokens_all.astype(F32)
        unit_one, _ = normed(inputs)
        me_dp = lax.axis_index("dp").astype(jnp.int32)[None]
        first_low = (unit_one * gain_one + shift_one).astype(BF)
        ids = (me_seq * heads + jnp.arange(heads) + 1).astype(F32)
        slopes = 2.0 ** (-8.0 * ids / HEADS)
        row, col = segments.reshape(1, length), segments.reshape(length, 1)
        ready = (first_low, grad_output, qkv_shift, slopes, row, col, o_shift, u_own, d_shift)
        ready = lax.optimization_barrier(ready)
        first_low, grad_output, qkv_shift, slopes, row, col, o_shift, u_own, d_shift = ready
        qkv, qkv_full, out_half = qkv_of(me_dp, q_pieces, first_low, qkv_shift, head_cols)
        if seq == 2:
            out_parts = [out_half, trade(out_half)]
            me_parts = jnp.stack([me_seq, me_seq, 1 - me_seq]).astype(jnp.int32)
        else:
            out_parts = [lax.all_gather(out_half, "seq", axis=1, tiled=True)]
            me_parts = jnp.stack([me_seq, 0]).astype(jnp.int32)

        mixed_own = attend(slopes, row, col, qkv, range(pairs))
        if seq == 2:
            mixed_parts = [mixed_own, trade(mixed_own)]
        else:
            mixed_parts = [lax.all_gather(mixed_own, "seq", axis=1, tiled=True)]
        mixed, middle, second_low = middle_of(
            me_parts, mixed_parts, out_parts, tokens_all, o_shift, gain_two, shift_two
        )
        activated, hidden_slope, up_full = up_of(me_dp, up_pieces, second_low, u_own)

        (down_sum,) = scatter_grads([activated], [grad_output], dp, (0, 1))
        g_hidden, up_bias_sum, down_full, z_own = back_of(
            me_dp, down_pieces, grad_output, hidden_slope, up_full
        )
        (up_sum,) = scatter_grads([second_low], [g_hidden], dp, (0, 1))
        if seq == 2:
            z_other = trade(z_own)
        else:
            z_other = lax.psum(z_own.astype(F32), "seq") - z_own.astype(F32)
        g_middle, g_attn, g_mixed, turn_sums = turn_of(
            me_parts, z_own, z_other, middle, grad_output, gain_two, out_parts, head_cols
        )
        groups = [range(pairs // 2), range(pairs // 2, pairs)] if pairs > 1 else [range(pairs)]
        g_qkv = [attend_back(slopes, row, col, qkv, g_mixed, group) for group in groups]
        first_sum, out_sum = scatter_grads([first_low, mixed], [g_qkv[0], g_attn], dp, (0,), head_cols)
        qkv_sums = [first_sum] + [scatter_grads([first_low], [part], dp, (1,))[0] for part in g_qkv[1:]]
        g_qkv = jnp.concatenate(g_qkv, axis=1)
        g_first_part = dot(g_qkv, qkv_full, ((1,), (1,)))
        first_sums = (jnp.sum(g_first_part * unit_one, axis=0), jnp.sum(g_first_part, axis=0))
        g_first = seq_reduce(g_first_part.reshape(seq, local, width), seq, BF)
        unit_own, inverse_own = normed(tokens[0].astype(F32))
        g_middle_own = pick(g_middle.reshape(seq, local, width), me_seq, 0)
        input_grad = g_middle_own + norm_back(g_first, gain_one, unit_own, inverse_own)

        late, _ = lax.optimization_barrier((activated, g_qkv))
        lowered = matmul(late, down_full)
        lowered = lowered.reshape(seq, local, width)
        lowered = seq_reduce(lowered, seq, F32)
        middle_own = pick(middle.reshape(seq, local, width), me_seq, 0)
        output = (middle_own + lowered + d_shift).astype(BF)[None]

        def to_rows(total):
            return seq_swap(total.reshape(seq, rows, -1), seq).transpose(1, 0, 2)

        up_rows = to_rows(up_sum).reshape(rows, seq, dp, hidden_rows)
        up_grad = up_rows.transpose(0, 2, 1, 3).reshape(rows, hidden)
        last_rows = to_rows(jnp.concatenate(qkv_sums + [out_sum], axis=1))
        out_grad = last_rows[:, :, 3 * head_cols :].reshape(rows, width)
        qkv_rows = last_rows[:, :, : 3 * head_cols].reshape(rows, seq, pairs, 3, PAIR)
        weight_grads = [qkv_rows[:, :, :, i].reshape(rows, width) for i in range(3)]

        def sums(matrix):
            return jnp.sum(matrix.astype(F32), axis=0)

        mine = jnp.arange(seq) == me_seq

        def heads_only(vector):
            return jnp.where(mine[:, None], vector.reshape(1, -1), 0.0).reshape(-1)

        share = 1.0 / seq
        qkv_columns = sums(g_qkv).reshape(pairs, 3, PAIR)
        up_bias_grad = jnp.where(
            mine[None, :, None], up_bias_sum.reshape(dp, 1, hidden_rows), 0.0
        )
        vectors = [
            heads_only(qkv_columns[:, 0]), heads_only(qkv_columns[:, 2]), turn_sums[2] * share,
            up_bias_grad, sums(cotangent[0]), *first_sums,
            turn_sums[0] * share, turn_sums[1] * share,
        ]
        packed = jnp.concatenate(
            [v.reshape(dp, seq, m) for v, m in zip(vectors, small_sizes)], axis=2
        ).reshape(dp, seq * sum(small_sizes) // 128, 128)
        if boxed(dp):
            small_sum = scatter_far(scatter_near(packed, dp, 0), dp)
        else:
            small_sum = lax.psum_scatter(packed, "dp", scatter_dimension=0, tiled=False)
        small_grad = seq_reduce(small_sum.reshape(seq, -1), seq, F32)
        small_grads = [
            small_grad[offsets[i] : offsets[i] + small_sizes[i]] for i in range(9)
        ]
        return (
            output, input_grad[None], *weight_grads, out_grad, up_grad, down_sum, *small_grads
        )

    return body


def solution(mesh):
    both = ("dp", "seq")
    matrix, vector = P(both, None), P(both)
    dp, seq = mesh.shape["dp"], mesh.shape["seq"]
    layer = make_body(dp, seq)

    return jax.shard_map(
        layer,
        mesh=mesh,
        in_specs=(P("dp", "seq", None), P("dp", None), P("dp", "seq", None))
        + (matrix,) * 6
        + (vector,) * 9,
        out_specs=(P("dp", "seq", None),) * 2 + (matrix,) * 6 + (vector,) * 9,
        check_vma=False,
    )
```

```python
import functools

import jax
import jax.numpy as jnp
from jax import lax
from jax.experimental import pallas as pl
from jax.experimental.pallas import tpu as pltpu
from jax.sharding import PartitionSpec as P


HEADS = 16
HEAD_DIM = 64
EPS = 1e-05
FAR = 1e30
BLOCK = 256
REACH = 512
BF = jnp.bfloat16
F32 = jnp.float32


def dot(left, right, contract):
    return lax.dot_general(left, right, (contract, ((), ())), preferred_element_type=F32)


def matmul(left, right):
    return dot(left, right, ((1,), (0,)))


def pick(array, index, axis):
    return lax.dynamic_index_in_dim(array, index, axis, keepdims=False)


def trade(array):
    return lax.ppermute(array, "seq", [(0, 1), (1, 0)])


def seq_gather(block, seq):
    if seq == 2:
        other = trade(block)
        first = lax.axis_index("seq") == 0
        return jnp.where(first, jnp.stack([block, other]), jnp.stack([other, block]))
    return lax.all_gather(block, "seq", axis=0)


def seq_swap(blocks, seq):
    if seq == 2:
        me = lax.axis_index("seq")
        own, other = pick(blocks, me, 0), trade(pick(blocks, 1 - me, 0))
        return jnp.where(me == 0, jnp.stack([own, other]), jnp.stack([other, own]))
    return lax.all_to_all(blocks, "seq", 0, 0)


def seq_reduce(blocks, seq, send):
    if seq == 2:
        me = lax.axis_index("seq")
        other = trade(pick(blocks, 1 - me, 0).astype(send))
        return pick(blocks, me, 0).astype(F32) + other.astype(F32)
    return lax.psum_scatter(blocks.astype(F32), "seq", scatter_dimension=0, tiled=False)


def flip(array, bits, count):
    return lax.ppermute(array, "dp", [(i, i ^ bits) for i in range(count)])


def boxed(count):
    return count == 16


def vmem_specs(count):
    return [pl.BlockSpec(memory_space=pltpu.VMEM)] * count


def split_kernel(me_ref, *refs):
    weights, up_ref, targets = refs[:4], refs[4], refs[5:]
    me, cols = me_ref[0], targets[0].shape[1] // 4
    tile = PAIR
    for away in range(2):
        first_ref, up_out = targets[away], targets[2 + away]
        base, start = (me ^ away) * cols, 0
        for colour in range(2):
            for at in range(colour * cols // 2, (colour + 1) * cols // 2, PAIR):
                for weight in weights[:3]:
                    column = pl.multiple_of(base + at, PAIR)
                    first_ref[:, start : start + PAIR] = weight[:, pl.ds(column, PAIR)]
                    start += PAIR
            column = pl.multiple_of(base + colour * (cols // 2), cols // 2)
            first_ref[:, start : start + cols // 2] = weights[3][:, pl.ds(column, cols // 2)]
            start += cols // 2
        for at in range(0, up_out.shape[1], tile):
            column = pl.multiple_of(2 * at + (me ^ away) * tile, tile)
            up_out[:, at : at + tile] = up_ref[:, pl.ds(column, tile)]


def split_weights(me, weights, up_weight):
    rows, width = weights[0].shape
    shapes = [(rows, 2 * width)] * 2 + [(rows, up_weight.shape[1] // 2)] * 2
    return pl.pallas_call(
        split_kernel,
        in_specs=[pl.BlockSpec(memory_space=pltpu.SMEM)] + vmem_specs(5),
        out_specs=vmem_specs(4),
        out_shape=[jax.ShapeDtypeStruct(shape, BF) for shape in shapes],
    )(me.astype(jnp.int32)[None], *weights, up_weight)


def two_rows(own, other, me):
    return jnp.where(
        me == 0, jnp.concatenate([own, other], axis=0), jnp.concatenate([other, own], axis=0)
    )


def pack_kernel(*refs):
    slots, outs = refs[:-2], refs[-2:]
    half = outs[0].shape[2]
    for k, slot in enumerate(slots):
        for colour in range(2):
            outs[colour][k] = slot[:, colour * half : (colour + 1) * half]


def put_pieces(me, pieces, targets):
    low, side, far = me % 2, (me // 2) % 2, me // 4
    n_far, rows, _ = pieces[0].shape
    for colour in range(2):
        for late in range(2):
            for early in range(2):
                piece = pieces[4 * colour + 2 * late + early]
                away = (early, late) if colour == 0 else (late, early)
                for k in range(n_far):
                    block = (far ^ k) * 4 + (side ^ away[1]) * 2 + (low ^ away[0])
                    at = pl.multiple_of(block * rows, rows)
                    start = 0
                    for ref, column, width in targets:
                        half = width // 2
                        first = column + colour * half
                        ref[pl.ds(at, rows), first : first + half] = piece[k, :, start : start + half]
                        start += half


def whole_spec(array):
    return pl.BlockSpec(array.shape, lambda i, *_: (0,) * array.ndim)


def gather_blocks(block, widths, count, after=None):
    rows, half = block.shape[0], block.shape[1] // 2
    if not boxed(count) or any(w % 256 for w in widths):
        whole = lax.all_gather(block, "dp", axis=0, tiled=True)
        starts = [sum(widths[:i]) // 2 for i in range(len(widths))]
        return [
            jnp.concatenate(
                [whole[:, at : at + w // 2], whole[:, half + at : half + at + w // 2]], axis=1
            )
            for at, w in zip(starts, widths)
        ], block
    n_far = count // 4
    if after is not None:
        block, _ = lax.optimization_barrier((block, after))
    slots = [block] + [flip(block, 4 * k, count) for k in range(1, n_far)]
    fars = pl.pallas_call(
        pack_kernel,
        in_specs=vmem_specs(n_far),
        out_specs=vmem_specs(2),
        out_shape=[jax.ShapeDtypeStruct((n_far, rows, half), block.dtype)] * 2,
    )(*slots)
    pieces = []
    for colour, far in enumerate(fars):
        first, second = (1, 2) if colour == 0 else (2, 1)
        got = flip(far, first, count)
        pieces += [far, got, flip(far, second, count)]
        pieces += [flip(got, second, count)]
    return pieces, slots[-1]


def gather_small(block, count):
    if not boxed(count):
        return lax.all_gather(block, "dp", axis=0)
    near = jnp.stack([block, flip(block, 1, count)])
    near = jnp.stack([near, flip(near, 2, count)])
    whole = jnp.stack([near] + [flip(near, 4 * k, count) for k in range(1, count // 4)]).reshape((count,) + block.shape)
    ids = jnp.arange(count)
    order = ((ids[:, None] ^ lax.axis_index("dp")) == ids[None, :]).astype(F32)
    return jnp.sum(order.reshape(count, count, 1, 1) * whole[None], axis=1)


FAR_ORDER = (0, 2, 1, 3)


def far_of(far, place):
    return far ^ ((place & 1) * 2 + place // 2)


def add_low(a, b):
    return (a.astype(F32) + b.astype(F32)).astype(b.dtype)


def scatter_near(grads, count, colour):
    me = lax.axis_index("dp")
    side, low = (me // 2) % 2, me % 2
    box = grads.reshape((count // 4, 2, 2) + grads.shape[1:])
    if colour == 0:
        order = ((1, 2, side), (1, 1, low))
    else:
        order = ((2, 1, low), (1, 2, side))
    for axis, bit, mine in order:
        got = flip(pick(box, 1 - mine, axis), bit, count)
        box = add_low(pick(box, mine, axis), got)
    return box


def scatter_far(box, count):
    far = lax.axis_index("dp") // 4
    total = pick(box, far, 0).astype(F32)
    for k in range(1, count // 4):
        total = total + flip(pick(box, far ^ k, 0), 4 * k, count).astype(F32)
    return total


def grad_kernel(widths, ways, me_ref, *refs):
    n = len(widths)
    lefts, rights, outs, scratch = refs[:n], refs[n : 2 * n], refs[2 * n : -1], refs[-1]
    low, side = me_ref[0] % 2, (me_ref[0] // 2) % 2
    rows, start = scratch.shape[1] // 4, 0
    for left, right, width in zip(lefts, rights, widths):
        for away in range(2):
            at = pl.multiple_of((side ^ away) * 2 * rows, 2 * rows)
            if rows % 128:
                part = left[:, pl.ds(at, 2 * rows)]
                turned = jnp.concatenate([part[:, rows:], part[:, :rows]], axis=1)
                scratch[:, 2 * away * rows : 2 * (away + 1) * rows] = jnp.where(low == 0, part, turned)
            else:
                for step in range(2):
                    at_low = pl.multiple_of(at + (low ^ step) * rows, rows)
                    scratch[:, (2 * away + step) * rows : (2 * away + step + 1) * rows] = left[
                        :, pl.ds(at_low, rows)
                    ]
        grads = dot(scratch[...], right[...], ((0,), (0,)))
        for side_away in range(2):
            for low_away in range(2):
                at = (2 * side_away + low_away) * rows
                for way, (colour, low_column, high_column) in enumerate(ways):
                    first, second = (side_away, low_away) if colour == 0 else (low_away, side_away)
                    lo, hi = max(start, low_column), min(start + width, high_column)
                    outs[2 * way + first][second, 0, :, lo - low_column : hi - low_column] = grads[
                        at : at + rows, lo - start : hi - start
                    ].astype(BF)
        start += width


def grad_blocks(lefts, rights, widths, column, count, ways):
    length, n_far = lefts[0].shape[0], count // 4
    depth = lefts[0].shape[1] // n_far
    shapes = [(2, n_far, depth // 4, high - low) for _, low, high in ways for _ in range(2)]
    in_specs = [pl.BlockSpec((length, depth), lambda k, me: (0, far_of(me[0] // 4, k))) for _ in lefts]
    in_specs += [pl.BlockSpec((length, w), lambda k, me: (0, 0)) for w in widths]
    if column:
        in_specs[-1] = pl.BlockSpec((length, widths[-1]), lambda k, me: (0, me[1]))
    me = [lax.axis_index("dp").astype(jnp.int32), lax.axis_index("seq").astype(jnp.int32)]
    return pl.pallas_call(
        functools.partial(grad_kernel, widths, ways),
        grid_spec=pltpu.PrefetchScalarGridSpec(
            num_scalar_prefetch=1,
            grid=(n_far,),
            in_specs=in_specs,
            out_specs=[
                pl.BlockSpec((2, 1) + shape[2:], lambda k, me: (0, k, 0, 0)) for shape in shapes
            ],
            scratch_shapes=[pltpu.VMEM((length, depth), BF)],
        ),
        out_shape=[jax.ShapeDtypeStruct(shape, BF) for shape in shapes],
    )(jnp.stack(me), *lefts, *rights)


def scatter_grads(lefts, rights, count, colours, column=0, stepwise=False):
    widths = [r.shape[1] for r in rights]
    if column:
        widths[-1] = column
    if not boxed(count) or any(w % 128 for w in widths) or any(a.shape[1] % (64 * count) for a in lefts):
        if column:
            last = lax.dynamic_slice_in_dim(
                rights[-1], lax.axis_index("seq") * column, column, 1
            )
            rights = rights[:-1] + [last]
        return [
            lax.psum_scatter(dot(a, b, ((0,), (0,))), "dp", scatter_dimension=0, tiled=True)
            for a, b in zip(lefts, rights)
        ]
    step = sum(widths) // len(colours)
    ways = [(colour, i * step, (i + 1) * step) for i, colour in enumerate(colours)]
    grads = grad_blocks(lefts, rights, widths, column, count, ways)
    ends = []
    for way, colour in enumerate(colours):
        keep, give = grads[2 * way : 2 * way + 2]
        first, second = (2, 1) if colour == 0 else (1, 2)
        got = flip(give, first, count)
        late = flip(add_low(keep[1], got[1]), second, count)
        ends.append((add_low(keep[0], got[0]), late))

    def joined(at, stop, kind):
        parts = [k[at:stop].astype(F32) + l[at:stop].astype(F32) for k, l in ends]
        return jnp.concatenate(parts, axis=2).astype(kind)

    if stepwise:
        got = flip(joined(2, 4, BF), 4, count)
        keep = joined(0, 2, BF)
        last = flip(add_low(keep[1], got[1]), 8, count)
        total = keep[0].astype(F32) + got[0].astype(F32) + last.astype(F32)
    else:
        total = joined(0, 1, F32)[0]
        for place in range(1, 4):
            part = joined(place, place + 1, BF)[0]
            k = FAR_ORDER[place]
            total = total + flip(part, 4 * k, count).astype(F32)
    sums, start = [], 0
    for width in widths:
        sums.append(total[:, start : start + width])
        start += width
    return sums


PAIR = 2 * HEAD_DIM


def window(block):
    return max(0, block - REACH // BLOCK) * BLOCK, (block + 1) * BLOCK


def distances(row_ref, col_ref, block, out_ref):
    start, stop = window(block)
    shape = (stop - start, BLOCK)
    key = lax.broadcasted_iota(jnp.int32, shape, 0) + start
    query = lax.broadcasted_iota(jnp.int32, shape, 1) + block * BLOCK
    same = col_ref[start:stop, :] == row_ref[:, block * BLOCK : (block + 1) * BLOCK]
    out_ref[...] = jnp.where((query >= key) & same, (query - key).astype(F32), FAR)


def all_distances(row_ref, col_ref, n_blocks, near_refs, far_ref):
    @pl.when(pl.program_id(0) == 0)
    def _():
        for block in range(n_blocks):
            wide = block - REACH // BLOCK
            target = far_ref.at[wide] if wide >= 0 else near_refs[block]
            distances(row_ref, col_ref, block, target)


def each_block(n_blocks, near_refs, far_ref, work):
    back = REACH // BLOCK
    for block in range(back):
        start, stop = window(block)
        work(block * BLOCK, start, stop - start, near_refs[block])

    for block in range(back, n_blocks):
        work(block * BLOCK, block * BLOCK - REACH, REACH + BLOCK, far_ref.at[block - back])


def chances_of(query, key, far, slope):
    scores = dot(key, query, ((1,), (1,))) - slope * far
    top = jnp.max(scores, axis=0, keepdims=True)
    grown = jnp.exp(scores - top)
    return grown * (1.0 / jnp.sum(grown, axis=0, keepdims=True))


def attend_kernel(n_blocks, first_ref, slope_ref, row_ref, col_ref, qkv_ref, o_ref, far_ref, *near_refs):
    pair = pl.program_id(0) + first_ref[0]
    all_distances(row_ref, col_ref, n_blocks, near_refs, far_ref)
    left = lax.broadcasted_iota(jnp.int32, (BLOCK, PAIR), 1) < HEAD_DIM

    def work(at, start, keys, distance_ref):
        rows, cols = pl.ds(at, BLOCK), pl.ds(start, keys)
        query = qkv_ref[rows, :PAIR] * BF(HEAD_DIM**-0.5)
        key, value = qkv_ref[cols, PAIR : 2 * PAIR], qkv_ref[cols, 2 * PAIR :]
        parts = []
        for side in range(2):
            mine = jnp.where(left if side == 0 else ~left, query, 0)
            share = chances_of(mine, key, distance_ref[...], slope_ref[2 * pair + side]).astype(BF)
            parts.append(dot(share, value, ((0,), (0,))))
        o_ref[rows, :] = jnp.where(left, parts[0], parts[1]).astype(BF)

    each_block(n_blocks, near_refs, far_ref, work)


def attend_back_kernel(
    n_blocks, first_ref, slope_ref, row_ref, col_ref, qkv_ref, g_ref, d_ref, k_sum, v_sum, far_ref, *near_refs
):
    pair = pl.program_id(0) + first_ref[0]
    all_distances(row_ref, col_ref, n_blocks, near_refs, far_ref)
    left = lax.broadcasted_iota(jnp.int32, (BLOCK, PAIR), 1) < HEAD_DIM
    scale = HEAD_DIM**-0.5

    def work(at, start, keys, distance_ref):
        rows, cols = pl.ds(at, BLOCK), pl.ds(start, keys)
        wide = lax.broadcasted_iota(jnp.int32, (keys, PAIR), 1) < HEAD_DIM
        query = qkv_ref[rows, :PAIR] * BF(scale)
        grad = g_ref[rows, :]
        key, value = qkv_ref[cols, PAIR : 2 * PAIR], qkv_ref[cols, 2 * PAIR :]
        dq, dk, dv = [], [], []
        for side in range(2):
            keep = left if side == 0 else ~left
            chances = chances_of(
                jnp.where(keep, query, 0), key, distance_ref[...], slope_ref[2 * pair + side]
            )
            g_chances = dot(value, jnp.where(keep, grad, 0), ((1,), (1,)))
            product = chances * g_chances
            inner = jnp.sum(product, axis=0, keepdims=True)
            g_scores = (product - chances * inner).astype(BF)
            dv.append(matmul(chances.astype(BF), grad))
            dk.append(matmul(g_scores, query))
            dq.append(dot(g_scores, key, ((0,), (0,))))
        d_ref[rows, :PAIR] = (jnp.where(left, dq[0], dq[1]) * scale).astype(BF)
        dk, dv = jnp.where(wide, dk[0], dk[1]), jnp.where(wide, dv[0], dv[1])
        old = keys - BLOCK
        if old:
            k_sum[pl.ds(start, old), :] += dk[:old]
            v_sum[pl.ds(start, old), :] += dv[:old]
        k_sum[rows, :] = dk[old:]
        v_sum[rows, :] = dv[old:]

    each_block(n_blocks, near_refs, far_ref, work)
    d_ref[:, PAIR : 2 * PAIR] = k_sum[...].astype(BF)
    d_ref[:, 2 * PAIR :] = v_sum[...].astype(BF)


def distance_scratch(length):
    back = REACH // BLOCK
    near = [pltpu.VMEM((window(block)[1] - window(block)[0], BLOCK), F32) for block in range(back)]
    return [pltpu.VMEM((length // BLOCK - back, REACH + BLOCK, BLOCK), F32)] + near


def attend_call(kernel, slopes, row, col, arrays, widths, out_width, sums, pairs):
    length = row.shape[1]
    in_specs = [
        pl.BlockSpec(memory_space=pltpu.SMEM),
        pl.BlockSpec((1, length), lambda p, first: (0, 0)),
        pl.BlockSpec((length, 1), lambda p, first: (0, 0)),
    ] + [pl.BlockSpec((length, w), lambda p, first: (0, p + first[0])) for w in widths]
    return pl.pallas_call(
        functools.partial(kernel, length // BLOCK),
        grid_spec=pltpu.PrefetchScalarGridSpec(
            num_scalar_prefetch=1,
            grid=(len(pairs),),
            in_specs=in_specs,
            out_specs=pl.BlockSpec((length, out_width), lambda p, first: (0, p)),
            scratch_shapes=[pltpu.VMEM((length, PAIR), F32)] * sums + distance_scratch(length),
        ),
        out_shape=jax.ShapeDtypeStruct((length, len(pairs) * out_width), BF),
    )(jnp.full((1,), pairs[0], jnp.int32), slopes, row, col, *arrays)


def attend(slopes, row, col, qkv, pairs):
    return attend_call(attend_kernel, slopes, row, col, [qkv], [3 * PAIR], PAIR, 0, pairs)


def attend_back(slopes, row, col, qkv, grads, pairs):
    return attend_call(attend_back_kernel, slopes, row, col, [qkv, grads], [3 * PAIR, PAIR], 3 * PAIR, 2, pairs)


def normed(matrix):
    centred = matrix - jnp.mean(matrix, axis=-1, keepdims=True)
    spread = jnp.mean(centred * centred, axis=-1, keepdims=True)
    inverse = lax.rsqrt(spread + EPS)
    return centred * inverse, inverse


def norm_back(grad, gain, unit, inverse):
    scaled = grad * gain
    return inverse * (
        scaled
        - jnp.mean(scaled, axis=-1, keepdims=True)
        - unit * jnp.mean(scaled * unit, axis=-1, keepdims=True)
    )


def gelu_and_slope(u):
    c = 0.7978845608
    square = u * u
    t = jnp.tanh(u * (c + (c * 0.044715) * square))
    half = 0.5 + 0.5 * t
    slope = half + (u - u * (t * t)) * (0.5 * c + (1.5 * c * 0.044715) * square)
    return u * half, slope


ROWS = 256
COLS = 512


def middle_kernel(n, me_ref, *refs):
    mixed_parts, weights = refs[:n], refs[n : 2 * n]
    x_ref, shift_ref, gain_ref, bias_ref, mixed_ref, middle_ref, low_ref = refs[2 * n :]
    for i in range(n):
        width = mixed_parts[i].shape[1]
        at = pl.multiple_of(me_ref[1 + i] * width, width)
        mixed_ref[:, pl.ds(at, width)] = mixed_parts[i][...]
    mixed = mixed_ref[...]
    for i in range(n):
        width = weights[i].shape[1]
        at = pl.multiple_of(me_ref[1 + i] * width, width)
        middle_ref[:, pl.ds(at, width)] = matmul(mixed, weights[i][...])
    middle = x_ref[...].astype(F32) + middle_ref[...] + shift_ref[...]
    middle_ref[...] = middle
    unit, _ = normed(middle)
    low_ref[...] = (unit * gain_ref[...] + bias_ref[...]).astype(BF)


def middle_of(me, mixed_parts, weights, inputs, shift, gain, bias):
    n, (length, width) = len(weights), inputs.shape
    rows = lambda w: pl.BlockSpec((ROWS, w), lambda i, me: (i, 0))
    whole = lambda r, w: pl.BlockSpec((r, w), lambda i, me: (0, 0))
    return pl.pallas_call(
        functools.partial(middle_kernel, n),
        grid_spec=pltpu.PrefetchScalarGridSpec(
            num_scalar_prefetch=1,
            grid=(length // ROWS,),
            in_specs=[rows(p.shape[1]) for p in mixed_parts]
            + [whole(*w.shape) for w in weights]
            + [rows(width)]
            + [whole(1, width)] * 3,
            out_specs=[rows(width)] * 3,
        ),
        out_shape=[jax.ShapeDtypeStruct((length, width), t) for t in (BF, F32, BF)],
    )(me, *mixed_parts, *weights, inputs, shift[None], gain[None], bias[None])


def qkv_kernel(me_ref, *refs):
    pieces, (low_ref, bias_ref, qkv_ref, full_ref, out_ref, scratch) = refs[:8], refs[8:]
    step = pl.program_id(0)
    width = scratch.shape[1]

    @pl.when(step == 0)
    def _():
        put_pieces(me_ref[0], pieces, [(scratch, 0, width), (out_ref, 0, out_ref.shape[1])])

    cols = qkv_ref.shape[1]
    weight = scratch[:, pl.ds(pl.multiple_of(step * cols, cols), cols)]
    full_ref[...] = weight
    qkv_ref[...] = (matmul(low_ref[...], weight) + bias_ref[...]).astype(BF)


def qkv_of(me, pieces, first_low, bias, head_cols):
    if len(pieces) == 2:
        return (matmul(first_low, pieces[0]) + bias).astype(BF), *pieces
    length, width = first_low.shape
    cols = pl.BlockSpec((length, head_cols), lambda i, me: (0, i))
    full = pl.BlockSpec((width, head_cols), lambda i, me: (0, i))
    return pl.pallas_call(
        qkv_kernel,
        grid_spec=pltpu.PrefetchScalarGridSpec(
            num_scalar_prefetch=1,
            grid=(3,),
            in_specs=[whole_spec(p) for p in pieces]
            + [whole_spec(first_low), pl.BlockSpec((1, head_cols), lambda i, me: (0, i))],
            out_specs=[cols, full, pl.BlockSpec((width, head_cols), lambda i, me: (0, 0))],
            scratch_shapes=[pltpu.VMEM((width, 3 * head_cols), BF)],
        ),
        out_shape=[
            jax.ShapeDtypeStruct((length, 3 * head_cols), BF),
            jax.ShapeDtypeStruct((width, 3 * head_cols), BF),
            jax.ShapeDtypeStruct((width, head_cols), BF),
        ],
    )(me, *pieces, first_low, bias[None])


def up_kernel(me_ref, *refs):
    pieces, (low_ref, bias_ref, act_ref, slope_ref, full_ref, scratch) = refs[:8], refs[8:]
    step = pl.program_id(0)

    @pl.when(step == 0)
    def _():
        put_pieces(me_ref[0], pieces, [(scratch, 0, scratch.shape[1])])

    cols = act_ref.shape[1]
    weight = scratch[:, pl.ds(pl.multiple_of(step * cols, cols), cols)]
    full_ref[...] = weight
    for at in range(0, act_ref.shape[0], ROWS):
        rows = slice(at, at + ROWS)
        act, slope = gelu_and_slope(matmul(low_ref[rows, :], weight) + bias_ref[...])
        act_ref[rows, :] = act.astype(BF)
        slope_ref[rows, :] = slope.astype(BF)


def up_of(me, pieces, second_low, bias):
    if len(pieces) == 1:
        act, slope = gelu_and_slope(matmul(second_low, pieces[0]) + bias)
        return act.astype(BF), slope.astype(BF), pieces[0]
    length, width = second_low.shape
    hidden = bias.shape[0]
    cols = pl.BlockSpec((length, COLS), lambda i, me: (0, i))
    return pl.pallas_call(
        up_kernel,
        grid_spec=pltpu.PrefetchScalarGridSpec(
            num_scalar_prefetch=1,
            grid=(hidden // COLS,),
            in_specs=[whole_spec(p) for p in pieces]
            + [whole_spec(second_low), pl.BlockSpec((1, COLS), lambda i, me: (0, i))],
            out_specs=[cols, cols, pl.BlockSpec((width, COLS), lambda i, me: (0, i))],
            scratch_shapes=[pltpu.VMEM((width, hidden), BF)],
        ),
        out_shape=[
            jax.ShapeDtypeStruct((length, hidden), BF),
            jax.ShapeDtypeStruct((length, hidden), BF),
            jax.ShapeDtypeStruct((width, hidden), BF),
        ],
    )(me, *pieces, second_low, bias[None])


def back_kernel(n_steps, me_ref, *refs):
    pieces, refs = refs[:8], refs[8:]
    dy_ref, slope_ref, up_ref, hidden_ref, sum_ref, full_ref, z_ref, scratch, held = refs
    step = pl.program_id(0)

    @pl.when(step == 0)
    def _():
        put_pieces(me_ref[0], pieces, [(scratch, 0, scratch.shape[1])])

    cols = hidden_ref.shape[1]

    @pl.when(step < n_steps)
    def _():
        at = pl.multiple_of(step * cols, cols)
        weight = scratch[pl.ds(at, cols), :]
        full_ref[...] = weight
        total = None
        for start in range(0, dy_ref.shape[0], ROWS):
            rows = slice(start, start + ROWS)
            g_act = dot(dy_ref[rows, :], weight, ((1,), (1,)))
            g_hidden = (g_act * slope_ref[rows, :].astype(F32)).astype(BF)
            hidden_ref[rows, :] = g_hidden
            held[rows, pl.ds(at, cols)] = g_hidden
            part = jnp.sum(g_hidden.astype(F32), axis=0, keepdims=True)
            total = part if total is None else total + part
        sum_ref[...] = total

    @pl.when(step >= n_steps)
    def _():
        z_ref[...] = dot(held[...], up_ref[...], ((1,), (1,))).astype(BF)


def back_of(me, pieces, grad_output, slope, up_full):
    length, width = grad_output.shape
    hidden = slope.shape[1]
    if len(pieces) == 1:
        g_hidden = (dot(grad_output, pieces[0], ((1,), (1,))) * slope.astype(F32)).astype(BF)
        z = dot(g_hidden, up_full, ((1,), (1,))).astype(BF)
        return g_hidden, jnp.sum(g_hidden.astype(F32), axis=0), pieces[0], z
    n_steps, n_late = hidden // COLS, width // ROWS
    early = lambda i: jnp.minimum(i, n_steps - 1)
    late = lambda i: jnp.maximum(i - n_steps, 0)
    cols = pl.BlockSpec((length, COLS), lambda i, me: (0, early(i)))
    return pl.pallas_call(
        functools.partial(back_kernel, n_steps),
        grid_spec=pltpu.PrefetchScalarGridSpec(
            num_scalar_prefetch=1,
            grid=(n_steps + n_late,),
            in_specs=[whole_spec(p) for p in pieces]
            + [whole_spec(grad_output), cols]
            + [pl.BlockSpec((ROWS, hidden), lambda i, me: (late(i), 0))],
            out_specs=[
                cols,
                pl.BlockSpec((1, COLS), lambda i, me: (0, early(i))),
                pl.BlockSpec((COLS, width), lambda i, me: (early(i), 0)),
                pl.BlockSpec((length, ROWS), lambda i, me: (0, late(i))),
            ],
            scratch_shapes=[pltpu.VMEM((hidden, width), BF), pltpu.VMEM((length, hidden), BF)],
        ),
        out_shape=[
            jax.ShapeDtypeStruct((length, hidden), BF),
            jax.ShapeDtypeStruct((1, hidden), F32),
            jax.ShapeDtypeStruct((hidden, width), BF),
            jax.ShapeDtypeStruct((length, width), BF),
        ],
    )(me, *pieces, grad_output, slope, up_full)


def turn_kernel(n, me_ref, *refs):
    own_ref, other_ref, middle_ref, dy_ref, gain_ref = refs[:5]
    weights = refs[5 : 5 + n]
    g_middle_ref, g_attn_ref, g_mixed_ref, sum_ref = refs[5 + n :]
    grad = own_ref[...].astype(F32) + other_ref[...].astype(F32)
    unit, inverse = normed(middle_ref[...])
    g_middle = dy_ref[...].astype(F32) + norm_back(grad, gain_ref[...], unit, inverse)
    g_middle_ref[...] = g_middle
    g_attn = g_middle.astype(BF)
    g_attn_ref[...] = g_attn
    total = None
    for i in range(n):
        width = weights[i].shape[1]
        at = pl.multiple_of(me_ref[1 + i] * width, width)
        part = dot(g_attn_ref[:, pl.ds(at, width)], weights[i][...], ((1,), (1,)))
        total = part if total is None else total + part
    g_mixed_ref[...] = total.astype(BF)
    sums = jnp.concatenate(
        [
            jnp.sum(v, axis=0, keepdims=True)
            for v in (grad * unit, grad, g_attn.astype(F32))
        ]
        + [jnp.zeros((5, grad.shape[1]), F32)],
        axis=0,
    )

    @pl.when(pl.program_id(0) == 0)
    def _():
        sum_ref[...] = sums

    @pl.when(pl.program_id(0) > 0)
    def _():
        sum_ref[...] += sums


def turn_of(me, own, other, middle, grad_output, gain, weights, head_cols):
    n, (length, width) = len(weights), middle.shape
    rows = lambda w: pl.BlockSpec((ROWS, w), lambda i, me: (i, 0))
    return pl.pallas_call(
        functools.partial(turn_kernel, n),
        grid_spec=pltpu.PrefetchScalarGridSpec(
            num_scalar_prefetch=1,
            grid=(length // ROWS,),
            in_specs=[rows(width)] * 4
            + [pl.BlockSpec((1, width), lambda i, me: (0, 0))]
            + [pl.BlockSpec((head_cols, w.shape[1]), lambda i, me: (me[0], 0)) for w in weights],
            out_specs=[rows(width), rows(width), rows(head_cols)]
            + [pl.BlockSpec((8, width), lambda i, me: (0, 0))],
        ),
        out_shape=[
            jax.ShapeDtypeStruct((length, width), F32),
            jax.ShapeDtypeStruct((length, width), BF),
            jax.ShapeDtypeStruct((length, head_cols), BF),
            jax.ShapeDtypeStruct((8, width), F32),
        ],
    )(me, own, other, middle, grad_output, gain[None], *weights)


def make_body(dp, seq):
    def body(
        tokens, segments, cotangent,
        query_weight, key_weight, value_weight, out_weight, up_weight, down_weight,
        query_bias, value_bias, out_bias, up_bias, down_bias,
        first_gain, first_shift, second_gain, second_shift,
    ):
        me_seq = lax.axis_index("seq")
        _, local, width = tokens.shape
        length = segments.shape[1]
        rows = query_weight.shape[0]
        hidden = up_weight.shape[1]
        hidden_rows = down_weight.shape[0]
        head_cols = width // seq
        heads = HEADS // seq
        hidden_cols = hidden // seq

        pairs = heads // 2
        small_params = (
            query_bias, value_bias, out_bias, up_bias, down_bias,
            first_gain, first_shift, second_gain, second_shift,
        )
        small_sizes = [v.shape[0] for v in small_params]
        offsets = [sum(small_sizes[:i]) for i in range(len(small_sizes))]

        def first_columns(s, colour):
            at, half = s * head_cols, head_cols // 2
            span = [pairs * colour // 2, pairs * (colour + 1) // 2] if pairs > 1 else [0, 1]
            parts = [
                w[:, at + p * PAIR : at + (p + 1) * PAIR]
                for p in range(*span)
                for w in (query_weight, key_weight, value_weight)
            ]
            if pairs == 1:
                joined = jnp.concatenate(parts, axis=1)
                parts = [joined[:, colour * 3 * half : (colour + 1) * 3 * half]]
            return parts + [out_weight[:, at + colour * half : at + (colour + 1) * half]]

        quick = seq == 2 and hidden_rows == PAIR and pairs > 1
        if quick:
            own, send, up_mine, up_send = split_weights(
                me_seq, (query_weight, key_weight, value_weight, out_weight), up_weight
            )
            first_own = two_rows(own, trade(send), me_seq)
        else:
            first_own = jnp.stack(
                [jnp.concatenate(first_columns(i, 0) + first_columns(i, 1), axis=1) for i in range(seq)]
            )
            first_own = seq_swap(first_own, seq).reshape(seq * rows, -1)
        q_pieces, mark = gather_blocks(first_own, [3 * head_cols, head_cols], dp)

        total = sum(small_sizes)
        small = sum(
            jnp.pad(v.astype(F32), (at, total - at - size))
            for v, at, size in zip(small_params, offsets, small_sizes)
        )
        small_all = seq_gather(small, seq).reshape(-1, 128)
        small_all = gather_small(small_all, dp).reshape(dp * seq, -1)

        if quick:
            up_own = two_rows(up_mine, trade(up_send), me_seq)
        else:
            up_own = up_weight.reshape(rows, dp, seq, hidden_rows).transpose(2, 0, 1, 3)
            up_own = seq_swap(up_own.reshape(seq, rows, hidden_cols), seq).reshape(seq * rows, -1)
        up_pieces, mark = gather_blocks(up_own, [hidden_cols], dp, mark)
        down_pieces, _ = gather_blocks(down_weight, [width], dp, mark)
        tokens_all = seq_gather(tokens[0], seq).reshape(length, width)
        grad_output = seq_gather(cotangent[0], seq).reshape(length, width)

        def small_of(index):
            return small_all[:, offsets[index] : offsets[index] + small_sizes[index]].reshape(-1)

        (q_shift, v_shift, o_shift, u_shift, d_shift, gain_one, shift_one, gain_two, shift_two) = [
            small_of(i) for i in range(9)
        ]

        def own_pairs(vector):
            return lax.dynamic_slice_in_dim(vector, me_seq * head_cols, head_cols, 0).reshape(pairs, PAIR)

        u_own = pick(u_shift.reshape(dp, seq, hidden_rows), me_seq, 1).reshape(-1)
        qkv_shift = jnp.stack(
            [own_pairs(q_shift), jnp.zeros((pairs, PAIR), F32), own_pairs(v_shift)], axis=1
        ).reshape(-1)

        inputs = tokens_all.astype(F32)
        unit_one, _ = normed(inputs)
        me_dp = lax.axis_index("dp").astype(jnp.int32)[None]
        first_low = (unit_one * gain_one + shift_one).astype(BF)
        ids = (me_seq * heads + jnp.arange(heads) + 1).astype(F32)
        slopes = 2.0 ** (-8.0 * ids / HEADS)
        row, col = segments.reshape(1, length), segments.reshape(length, 1)
        ready = (first_low, grad_output, qkv_shift, slopes, row, col, o_shift, u_own, d_shift)
        ready = lax.optimization_barrier(ready)
        first_low, grad_output, qkv_shift, slopes, row, col, o_shift, u_own, d_shift = ready
        qkv, qkv_full, out_half = qkv_of(me_dp, q_pieces, first_low, qkv_shift, head_cols)
        if seq == 2:
            out_parts = [out_half, trade(out_half)]
            me_parts = jnp.stack([me_seq, me_seq, 1 - me_seq]).astype(jnp.int32)
        else:
            out_parts = [lax.all_gather(out_half, "seq", axis=1, tiled=True)]
            me_parts = jnp.stack([me_seq, 0]).astype(jnp.int32)

        mixed_own = attend(slopes, row, col, qkv, range(pairs))
        if seq == 2:
            mixed_parts = [mixed_own, trade(mixed_own)]
        else:
            mixed_parts = [lax.all_gather(mixed_own, "seq", axis=1, tiled=True)]
        mixed, middle, second_low = middle_of(
            me_parts, mixed_parts, out_parts, tokens_all, o_shift, gain_two, shift_two
        )
        activated, hidden_slope, up_full = up_of(me_dp, up_pieces, second_low, u_own)

        (down_sum,) = scatter_grads([activated], [grad_output], dp, (0,), stepwise=True)
        g_hidden, up_bias_sum, down_full, z_own = back_of(
            me_dp, down_pieces, grad_output, hidden_slope, up_full
        )
        (up_sum,) = scatter_grads([second_low], [g_hidden], dp, (0, 1), stepwise=True)
        if seq == 2:
            z_other = trade(z_own)
        else:
            z_other = lax.psum(z_own.astype(F32), "seq") - z_own.astype(F32)
        g_middle, g_attn, g_mixed, turn_sums = turn_of(
            me_parts, z_own, z_other, middle, grad_output, gain_two, out_parts, head_cols
        )
        groups = [range(pairs // 2), range(pairs // 2, pairs)] if pairs > 1 else [range(pairs)]
        g_qkv = [attend_back(slopes, row, col, qkv, g_mixed, group) for group in groups]
        first_sum, out_sum = scatter_grads([first_low, mixed], [g_qkv[0], g_attn], dp, (0,), head_cols)
        qkv_sums = [first_sum] + [scatter_grads([first_low], [part], dp, (1,))[0] for part in g_qkv[1:]]
        g_qkv = jnp.concatenate(g_qkv, axis=1)
        g_first_part = dot(g_qkv, qkv_full, ((1,), (1,)))
        first_sums = (jnp.sum(g_first_part * unit_one, axis=0), jnp.sum(g_first_part, axis=0))
        g_first = seq_reduce(g_first_part.reshape(seq, local, width), seq, BF)
        unit_own, inverse_own = normed(tokens[0].astype(F32))
        g_middle_own = pick(g_middle.reshape(seq, local, width), me_seq, 0)
        input_grad = g_middle_own + norm_back(g_first, gain_one, unit_own, inverse_own)

        late, _ = lax.optimization_barrier((activated, g_qkv))
        lowered = matmul(late, down_full)
        lowered = lowered.reshape(seq, local, width)
        lowered = seq_reduce(lowered, seq, F32)
        middle_own = pick(middle.reshape(seq, local, width), me_seq, 0)
        output = (middle_own + lowered + d_shift).astype(BF)[None]

        def to_rows(total):
            return seq_swap(total.reshape(seq, rows, -1), seq).transpose(1, 0, 2)

        up_rows = to_rows(up_sum).reshape(rows, seq, dp, hidden_rows)
        up_grad = up_rows.transpose(0, 2, 1, 3).reshape(rows, hidden)
        last_rows = to_rows(jnp.concatenate(qkv_sums + [out_sum], axis=1))
        out_grad = last_rows[:, :, 3 * head_cols :].reshape(rows, width)
        qkv_rows = last_rows[:, :, : 3 * head_cols].reshape(rows, seq, pairs, 3, PAIR)
        weight_grads = [qkv_rows[:, :, :, i].reshape(rows, width) for i in range(3)]

        def sums(matrix):
            return jnp.sum(matrix.astype(F32), axis=0)

        mine = jnp.arange(seq) == me_seq

        def heads_only(vector):
            return jnp.where(mine[:, None], vector.reshape(1, -1), 0.0).reshape(-1)

        share = 1.0 / seq
        qkv_columns = sums(g_qkv).reshape(pairs, 3, PAIR)
        up_bias_grad = jnp.where(
            mine[None, :, None], up_bias_sum.reshape(dp, 1, hidden_rows), 0.0
        )
        vectors = [
            heads_only(qkv_columns[:, 0]), heads_only(qkv_columns[:, 2]), turn_sums[2] * share,
            up_bias_grad, sums(cotangent[0]), *first_sums,
            turn_sums[0] * share, turn_sums[1] * share,
        ]
        packed = jnp.concatenate(
            [v.reshape(dp, seq, m) for v, m in zip(vectors, small_sizes)], axis=2
        ).reshape(dp, seq * sum(small_sizes) // 128, 128)
        if boxed(dp):
            small_sum = scatter_far(scatter_near(packed, dp, 0), dp)
        else:
            small_sum = lax.psum_scatter(packed, "dp", scatter_dimension=0, tiled=False)
        small_grad = seq_reduce(small_sum.reshape(seq, -1), seq, F32)
        small_grads = [
            small_grad[offsets[i] : offsets[i] + small_sizes[i]] for i in range(9)
        ]
        return (
            output, input_grad[None], *weight_grads, out_grad, up_grad, down_sum, *small_grads
        )

    return body


def solution(mesh):
    both = ("dp", "seq")
    matrix, vector = P(both, None), P(both)
    dp, seq = mesh.shape["dp"], mesh.shape["seq"]
    layer = make_body(dp, seq)

    return jax.shard_map(
        layer,
        mesh=mesh,
        in_specs=(P("dp", "seq", None), P("dp", None), P("dp", "seq", None))
        + (matrix,) * 6
        + (vector,) * 9,
        out_specs=(P("dp", "seq", None),) * 2 + (matrix,) * 6 + (vector,) * 9,
        check_vma=False,
    )
```

```python
import functools

import jax
import jax.numpy as jnp
from jax import lax
from jax.experimental import pallas as pl
from jax.experimental.pallas import tpu as pltpu
from jax.sharding import PartitionSpec as P


HEADS = 16
HEAD_DIM = 64
EPS = 1e-05
FAR = 1e30
BLOCK = 256
REACH = 512
BF = jnp.bfloat16
F32 = jnp.float32


def dot(left, right, contract):
    return lax.dot_general(left, right, (contract, ((), ())), preferred_element_type=F32)


def matmul(left, right):
    return dot(left, right, ((1,), (0,)))


def pick(array, index, axis):
    return lax.dynamic_index_in_dim(array, index, axis, keepdims=False)


def trade(array):
    return lax.ppermute(array, "seq", [(0, 1), (1, 0)])


def seq_gather(block, seq):
    if seq == 2:
        other = trade(block)
        first = lax.axis_index("seq") == 0
        return jnp.where(first, jnp.stack([block, other]), jnp.stack([other, block]))
    return lax.all_gather(block, "seq", axis=0)


def seq_swap(blocks, seq):
    if seq == 2:
        me = lax.axis_index("seq")
        own, other = pick(blocks, me, 0), trade(pick(blocks, 1 - me, 0))
        return jnp.where(me == 0, jnp.stack([own, other]), jnp.stack([other, own]))
    return lax.all_to_all(blocks, "seq", 0, 0)


def seq_reduce(blocks, seq, send):
    if seq == 2:
        me = lax.axis_index("seq")
        other = trade(pick(blocks, 1 - me, 0).astype(send))
        return pick(blocks, me, 0).astype(F32) + other.astype(F32)
    return lax.psum_scatter(blocks.astype(F32), "seq", scatter_dimension=0, tiled=False)


def flip(array, bits, count):
    return lax.ppermute(array, "dp", [(i, i ^ bits) for i in range(count)])


def boxed(count):
    return count >= 4 and not count & (count - 1)


def vmem_specs(count):
    return [pl.BlockSpec(memory_space=pltpu.VMEM)] * count


def split_kernel(me_ref, *refs):
    weights, up_ref, targets = refs[:4], refs[4], refs[5:]
    me, cols = me_ref[0], targets[0].shape[1] // 4
    tile = PAIR
    for away in range(2):
        first_ref, up_out = targets[away], targets[2 + away]
        base, start = (me ^ away) * cols, 0
        for colour in range(2):
            for at in range(colour * cols // 2, (colour + 1) * cols // 2, PAIR):
                for weight in weights[:3]:
                    column = pl.multiple_of(base + at, PAIR)
                    first_ref[:, start : start + PAIR] = weight[:, pl.ds(column, PAIR)]
                    start += PAIR
            column = pl.multiple_of(base + colour * (cols // 2), cols // 2)
            first_ref[:, start : start + cols // 2] = weights[3][:, pl.ds(column, cols // 2)]
            start += cols // 2
        for at in range(0, up_out.shape[1], tile):
            column = pl.multiple_of(2 * at + (me ^ away) * tile, tile)
            up_out[:, at : at + tile] = up_ref[:, pl.ds(column, tile)]


def split_weights(me, weights, up_weight):
    rows, width = weights[0].shape
    shapes = [(rows, 2 * width)] * 2 + [(rows, up_weight.shape[1] // 2)] * 2
    return pl.pallas_call(
        split_kernel,
        in_specs=[pl.BlockSpec(memory_space=pltpu.SMEM)] + vmem_specs(5),
        out_specs=vmem_specs(4),
        out_shape=[jax.ShapeDtypeStruct(shape, BF) for shape in shapes],
    )(me.astype(jnp.int32)[None], *weights, up_weight)


def two_rows(own, other, me):
    return jnp.where(
        me == 0, jnp.concatenate([own, other], axis=0), jnp.concatenate([other, own], axis=0)
    )


def pack_kernel(*refs):
    slots, outs = refs[:-2], refs[-2:]
    half = outs[0].shape[2]
    for k, slot in enumerate(slots):
        for colour in range(2):
            outs[colour][k] = slot[:, colour * half : (colour + 1) * half]


def put_pieces(me, pieces, targets):
    low, side, far = me % 2, (me // 2) % 2, me // 4
    n_far, rows, _ = pieces[0].shape
    for colour in range(2):
        for late in range(2):
            for early in range(2):
                piece = pieces[4 * colour + 2 * late + early]
                away = (early, late) if colour == 0 else (late, early)
                for k in range(n_far):
                    block = (far ^ k) * 4 + (side ^ away[1]) * 2 + (low ^ away[0])
                    at = pl.multiple_of(block * rows, rows)
                    start = 0
                    for ref, column, width in targets:
                        half = width // 2
                        first = column + colour * half
                        ref[pl.ds(at, rows), first : first + half] = piece[k, :, start : start + half]
                        start += half


def whole_spec(array):
    return pl.BlockSpec(array.shape, lambda i, *_: (0,) * array.ndim)


def gather_blocks(block, widths, count, after=None):
    rows, half = block.shape[0], block.shape[1] // 2
    if not boxed(count) or any(w % 256 for w in widths):
        whole = lax.all_gather(block, "dp", axis=0, tiled=True)
        starts = [sum(widths[:i]) // 2 for i in range(len(widths))]
        return [
            jnp.concatenate(
                [whole[:, at : at + w // 2], whole[:, half + at : half + at + w // 2]], axis=1
            )
            for at, w in zip(starts, widths)
        ], block
    n_far = count // 4
    if after is not None:
        block, _ = lax.optimization_barrier((block, after))
    slots = [block] + [flip(block, 4 * k, count) for k in range(1, n_far)]
    fars = pl.pallas_call(
        pack_kernel,
        in_specs=vmem_specs(n_far),
        out_specs=vmem_specs(2),
        out_shape=[jax.ShapeDtypeStruct((n_far, rows, half), block.dtype)] * 2,
    )(*slots)
    pieces = []
    for colour, far in enumerate(fars):
        first, second = (1, 2) if colour == 0 else (2, 1)
        got = flip(far, first, count)
        pieces += [far, got, flip(far, second, count)]
        pieces += [flip(got, second, count)]
    return pieces, slots[-1]


def gather_small(block, count):
    if not boxed(count):
        return lax.all_gather(block, "dp", axis=0)
    near = jnp.stack([block, flip(block, 1, count)])
    near = jnp.stack([near, flip(near, 2, count)])
    whole = jnp.stack([near] + [flip(near, 4 * k, count) for k in range(1, count // 4)]).reshape((count,) + block.shape)
    ids = jnp.arange(count)
    order = ((ids[:, None] ^ lax.axis_index("dp")) == ids[None, :]).astype(F32)
    return jnp.sum(order.reshape(count, count, 1, 1) * whole[None], axis=1)


def add_low(a, b):
    return (a.astype(F32) + b.astype(F32)).astype(b.dtype)


def scatter_near(grads, count, colour):
    me = lax.axis_index("dp")
    side, low = (me // 2) % 2, me % 2
    box = grads.reshape((count // 4, 2, 2) + grads.shape[1:])
    if colour == 0:
        order = ((1, 2, side), (1, 1, low))
    else:
        order = ((2, 1, low), (1, 2, side))
    for axis, bit, mine in order:
        got = flip(pick(box, 1 - mine, axis), bit, count)
        box = add_low(pick(box, mine, axis), got)
    return box


def scatter_far(box, count):
    far = lax.axis_index("dp") // 4
    total = pick(box, far, 0).astype(F32)
    for k in range(1, count // 4):
        total = total + flip(pick(box, far ^ k, 0), 4 * k, count).astype(F32)
    return total


def grad_kernel(widths, ways, me_ref, *refs):
    n = len(widths)
    lefts, rights, outs, scratch = refs[:n], refs[n : 2 * n], refs[2 * n : -1], refs[-1]
    low, side = me_ref[0] % 2, (me_ref[0] // 2) % 2
    rows, start = scratch.shape[1] // 4, 0
    for left, right, width in zip(lefts, rights, widths):
        for away in range(2):
            at = pl.multiple_of((side ^ away) * 2 * rows, 2 * rows)
            if rows % 128:
                part = left[:, pl.ds(at, 2 * rows)]
                turned = jnp.concatenate([part[:, rows:], part[:, :rows]], axis=1)
                scratch[:, 2 * away * rows : 2 * (away + 1) * rows] = jnp.where(low == 0, part, turned)
            else:
                for step in range(2):
                    at_low = pl.multiple_of(at + (low ^ step) * rows, rows)
                    scratch[:, (2 * away + step) * rows : (2 * away + step + 1) * rows] = left[
                        :, pl.ds(at_low, rows)
                    ]
        grads = dot(scratch[...], right[...], ((0,), (0,)))
        for side_away in range(2):
            for low_away in range(2):
                at = (2 * side_away + low_away) * rows
                for way, (colour, low_column, high_column) in enumerate(ways):
                    first, second = (side_away, low_away) if colour == 0 else (low_away, side_away)
                    lo, hi = max(start, low_column), min(start + width, high_column)
                    outs[2 * way + first][second, 0, :, lo - low_column : hi - low_column] = grads[
                        at : at + rows, lo - start : hi - start
                    ].astype(BF)
        start += width


def grad_blocks(lefts, rights, widths, column, count, ways):
    length, n_far = lefts[0].shape[0], count // 4
    depth = lefts[0].shape[1] // n_far
    shapes = [(2, n_far, depth // 4, high - low) for _, low, high in ways for _ in range(2)]
    in_specs = [pl.BlockSpec((length, depth), lambda k, me: (0, (me[0] // 4) ^ k)) for _ in lefts]
    in_specs += [pl.BlockSpec((length, w), lambda k, me: (0, 0)) for w in widths]
    if column:
        in_specs[-1] = pl.BlockSpec((length, widths[-1]), lambda k, me: (0, me[1]))
    me = [lax.axis_index("dp").astype(jnp.int32), lax.axis_index("seq").astype(jnp.int32)]
    return pl.pallas_call(
        functools.partial(grad_kernel, widths, ways),
        grid_spec=pltpu.PrefetchScalarGridSpec(
            num_scalar_prefetch=1,
            grid=(n_far,),
            in_specs=in_specs,
            out_specs=[
                pl.BlockSpec((2, 1) + shape[2:], lambda k, me: (0, k, 0, 0)) for shape in shapes
            ],
            scratch_shapes=[pltpu.VMEM((length, depth), BF)],
        ),
        out_shape=[jax.ShapeDtypeStruct(shape, BF) for shape in shapes],
    )(jnp.stack(me), *lefts, *rights)


def scatter_grads(lefts, rights, count, colours, column=0):
    widths = [r.shape[1] for r in rights]
    if column:
        widths[-1] = column
    if not boxed(count) or any(w % 128 for w in widths) or any(a.shape[1] % (64 * count) for a in lefts):
        if column:
            last = lax.dynamic_slice_in_dim(
                rights[-1], lax.axis_index("seq") * column, column, 1
            )
            rights = rights[:-1] + [last]
        return [
            lax.psum_scatter(dot(a, b, ((0,), (0,))), "dp", scatter_dimension=0, tiled=True)
            for a, b in zip(lefts, rights)
        ]
    step = sum(widths) // len(colours)
    ways = [(colour, i * step, (i + 1) * step) for i, colour in enumerate(colours)]
    grads = grad_blocks(lefts, rights, widths, column, count, ways)
    ends = []
    for way, colour in enumerate(colours):
        keep, give = grads[2 * way : 2 * way + 2]
        first, second = (2, 1) if colour == 0 else (1, 2)
        got = flip(give, first, count)
        late = flip(add_low(keep[1], got[1]), second, count)
        ends.append((add_low(keep[0], got[0]), late))
    total = jnp.concatenate([k[0].astype(F32) + l[0].astype(F32) for k, l in ends], axis=1)
    for k in range(1, count // 4):
        part = jnp.concatenate([add_low(keep[k], late[k]) for keep, late in ends], axis=1)
        total = total + flip(part, 4 * k, count).astype(F32)
    sums, start = [], 0
    for width in widths:
        sums.append(total[:, start : start + width])
        start += width
    return sums


PAIR = 2 * HEAD_DIM


def window(block):
    return max(0, block - REACH // BLOCK) * BLOCK, (block + 1) * BLOCK


def distances(row_ref, col_ref, block, out_ref):
    start, stop = window(block)
    shape = (stop - start, BLOCK)
    key = lax.broadcasted_iota(jnp.int32, shape, 0) + start
    query = lax.broadcasted_iota(jnp.int32, shape, 1) + block * BLOCK
    same = col_ref[start:stop, :] == row_ref[:, block * BLOCK : (block + 1) * BLOCK]
    out_ref[...] = jnp.where((query >= key) & same, (query - key).astype(F32), FAR)


def all_distances(row_ref, col_ref, n_blocks, near_refs, far_ref):
    @pl.when(pl.program_id(0) == 0)
    def _():
        for block in range(n_blocks):
            wide = block - REACH // BLOCK
            target = far_ref.at[wide] if wide >= 0 else near_refs[block]
            distances(row_ref, col_ref, block, target)


def each_block(n_blocks, near_refs, far_ref, work):
    back = REACH // BLOCK
    for block in range(back):
        start, stop = window(block)
        work(block * BLOCK, start, stop - start, near_refs[block])

    for block in range(back, n_blocks):
        work(block * BLOCK, block * BLOCK - REACH, REACH + BLOCK, far_ref.at[block - back])


def chances_of(query, key, far, slope):
    scores = dot(key, query, ((1,), (1,))) - slope * far
    top = jnp.max(scores, axis=0, keepdims=True)
    grown = jnp.exp(scores - top)
    return grown * (1.0 / jnp.sum(grown, axis=0, keepdims=True))


def attend_kernel(n_blocks, first_ref, slope_ref, row_ref, col_ref, qkv_ref, o_ref, far_ref, *near_refs):
    pair = pl.program_id(0) + first_ref[0]
    all_distances(row_ref, col_ref, n_blocks, near_refs, far_ref)
    left = lax.broadcasted_iota(jnp.int32, (BLOCK, PAIR), 1) < HEAD_DIM

    def work(at, start, keys, distance_ref):
        rows, cols = pl.ds(at, BLOCK), pl.ds(start, keys)
        query = qkv_ref[rows, :PAIR] * BF(HEAD_DIM**-0.5)
        key, value = qkv_ref[cols, PAIR : 2 * PAIR], qkv_ref[cols, 2 * PAIR :]
        parts = []
        for side in range(2):
            mine = jnp.where(left if side == 0 else ~left, query, 0)
            share = chances_of(mine, key, distance_ref[...], slope_ref[2 * pair + side]).astype(BF)
            parts.append(dot(share, value, ((0,), (0,))))
        o_ref[rows, :] = jnp.where(left, parts[0], parts[1]).astype(BF)

    each_block(n_blocks, near_refs, far_ref, work)


def attend_back_kernel(
    n_blocks, first_ref, slope_ref, row_ref, col_ref, qkv_ref, g_ref, d_ref, k_sum, v_sum, far_ref, *near_refs
):
    pair = pl.program_id(0) + first_ref[0]
    all_distances(row_ref, col_ref, n_blocks, near_refs, far_ref)
    left = lax.broadcasted_iota(jnp.int32, (BLOCK, PAIR), 1) < HEAD_DIM
    scale = HEAD_DIM**-0.5

    def work(at, start, keys, distance_ref):
        rows, cols = pl.ds(at, BLOCK), pl.ds(start, keys)
        wide = lax.broadcasted_iota(jnp.int32, (keys, PAIR), 1) < HEAD_DIM
        query = qkv_ref[rows, :PAIR] * BF(scale)
        grad = g_ref[rows, :]
        key, value = qkv_ref[cols, PAIR : 2 * PAIR], qkv_ref[cols, 2 * PAIR :]
        dq, dk, dv = [], [], []
        for side in range(2):
            keep = left if side == 0 else ~left
            chances = chances_of(
                jnp.where(keep, query, 0), key, distance_ref[...], slope_ref[2 * pair + side]
            )
            g_chances = dot(value, jnp.where(keep, grad, 0), ((1,), (1,)))
            product = chances * g_chances
            inner = jnp.sum(product, axis=0, keepdims=True)
            g_scores = (product - chances * inner).astype(BF)
            dv.append(matmul(chances.astype(BF), grad))
            dk.append(matmul(g_scores, query))
            dq.append(dot(g_scores, key, ((0,), (0,))))
        d_ref[rows, :PAIR] = (jnp.where(left, dq[0], dq[1]) * scale).astype(BF)
        dk, dv = jnp.where(wide, dk[0], dk[1]), jnp.where(wide, dv[0], dv[1])
        old = keys - BLOCK
        if old:
            k_sum[pl.ds(start, old), :] += dk[:old]
            v_sum[pl.ds(start, old), :] += dv[:old]
        k_sum[rows, :] = dk[old:]
        v_sum[rows, :] = dv[old:]

    each_block(n_blocks, near_refs, far_ref, work)
    d_ref[:, PAIR : 2 * PAIR] = k_sum[...].astype(BF)
    d_ref[:, 2 * PAIR :] = v_sum[...].astype(BF)


def distance_scratch(length):
    back = REACH // BLOCK
    near = [pltpu.VMEM((window(block)[1] - window(block)[0], BLOCK), F32) for block in range(back)]
    return [pltpu.VMEM((length // BLOCK - back, REACH + BLOCK, BLOCK), F32)] + near


def attend_call(kernel, slopes, row, col, arrays, widths, out_width, sums, pairs):
    length = row.shape[1]
    in_specs = [
        pl.BlockSpec(memory_space=pltpu.SMEM),
        pl.BlockSpec((1, length), lambda p, first: (0, 0)),
        pl.BlockSpec((length, 1), lambda p, first: (0, 0)),
    ] + [pl.BlockSpec((length, w), lambda p, first: (0, p + first[0])) for w in widths]
    return pl.pallas_call(
        functools.partial(kernel, length // BLOCK),
        grid_spec=pltpu.PrefetchScalarGridSpec(
            num_scalar_prefetch=1,
            grid=(len(pairs),),
            in_specs=in_specs,
            out_specs=pl.BlockSpec((length, out_width), lambda p, first: (0, p)),
            scratch_shapes=[pltpu.VMEM((length, PAIR), F32)] * sums + distance_scratch(length),
        ),
        out_shape=jax.ShapeDtypeStruct((length, len(pairs) * out_width), BF),
    )(jnp.full((1,), pairs[0], jnp.int32), slopes, row, col, *arrays)


def attend(slopes, row, col, qkv, pairs):
    return attend_call(attend_kernel, slopes, row, col, [qkv], [3 * PAIR], PAIR, 0, pairs)


def attend_back(slopes, row, col, qkv, grads, pairs):
    return attend_call(attend_back_kernel, slopes, row, col, [qkv, grads], [3 * PAIR, PAIR], 3 * PAIR, 2, pairs)


def normed(matrix):
    centred = matrix - jnp.mean(matrix, axis=-1, keepdims=True)
    spread = jnp.mean(centred * centred, axis=-1, keepdims=True)
    inverse = lax.rsqrt(spread + EPS)
    return centred * inverse, inverse


def norm_back(grad, gain, unit, inverse):
    scaled = grad * gain
    return inverse * (
        scaled
        - jnp.mean(scaled, axis=-1, keepdims=True)
        - unit * jnp.mean(scaled * unit, axis=-1, keepdims=True)
    )


def gelu_and_slope(u):
    c = 0.7978845608
    square = u * u
    t = jnp.tanh(u * (c + (c * 0.044715) * square))
    half = 0.5 + 0.5 * t
    slope = half + (u - u * (t * t)) * (0.5 * c + (1.5 * c * 0.044715) * square)
    return u * half, slope


ROWS = 256
COLS = 512


def middle_kernel(n, me_ref, *refs):
    mixed_parts, weights = refs[:n], refs[n : 2 * n]
    x_ref, shift_ref, gain_ref, bias_ref, mixed_ref, middle_ref, low_ref = refs[2 * n :]
    for i in range(n):
        width = mixed_parts[i].shape[1]
        at = pl.multiple_of(me_ref[1 + i] * width, width)
        mixed_ref[:, pl.ds(at, width)] = mixed_parts[i][...]
    mixed = mixed_ref[...]
    for i in range(n):
        width = weights[i].shape[1]
        at = pl.multiple_of(me_ref[1 + i] * width, width)
        middle_ref[:, pl.ds(at, width)] = matmul(mixed, weights[i][...])
    middle = x_ref[...].astype(F32) + middle_ref[...] + shift_ref[...]
    middle_ref[...] = middle
    unit, _ = normed(middle)
    low_ref[...] = (unit * gain_ref[...] + bias_ref[...]).astype(BF)


def middle_of(me, mixed_parts, weights, inputs, shift, gain, bias):
    n, (length, width) = len(weights), inputs.shape
    rows = lambda w: pl.BlockSpec((ROWS, w), lambda i, me: (i, 0))
    whole = lambda r, w: pl.BlockSpec((r, w), lambda i, me: (0, 0))
    return pl.pallas_call(
        functools.partial(middle_kernel, n),
        grid_spec=pltpu.PrefetchScalarGridSpec(
            num_scalar_prefetch=1,
            grid=(length // ROWS,),
            in_specs=[rows(p.shape[1]) for p in mixed_parts]
            + [whole(*w.shape) for w in weights]
            + [rows(width)]
            + [whole(1, width)] * 3,
            out_specs=[rows(width)] * 3,
        ),
        out_shape=[jax.ShapeDtypeStruct((length, width), t) for t in (BF, F32, BF)],
    )(me, *mixed_parts, *weights, inputs, shift[None], gain[None], bias[None])


def qkv_kernel(me_ref, *refs):
    pieces, (low_ref, bias_ref, qkv_ref, full_ref, out_ref, scratch) = refs[:8], refs[8:]
    step = pl.program_id(0)
    width = scratch.shape[1]

    @pl.when(step == 0)
    def _():
        put_pieces(me_ref[0], pieces, [(scratch, 0, width), (out_ref, 0, out_ref.shape[1])])

    cols = qkv_ref.shape[1]
    weight = scratch[:, pl.ds(pl.multiple_of(step * cols, cols), cols)]
    full_ref[...] = weight
    qkv_ref[...] = (matmul(low_ref[...], weight) + bias_ref[...]).astype(BF)


def qkv_of(me, pieces, first_low, bias, head_cols):
    if len(pieces) == 2:
        return (matmul(first_low, pieces[0]) + bias).astype(BF), *pieces
    length, width = first_low.shape
    cols = pl.BlockSpec((length, head_cols), lambda i, me: (0, i))
    full = pl.BlockSpec((width, head_cols), lambda i, me: (0, i))
    return pl.pallas_call(
        qkv_kernel,
        grid_spec=pltpu.PrefetchScalarGridSpec(
            num_scalar_prefetch=1,
            grid=(3,),
            in_specs=[whole_spec(p) for p in pieces]
            + [whole_spec(first_low), pl.BlockSpec((1, head_cols), lambda i, me: (0, i))],
            out_specs=[cols, full, pl.BlockSpec((width, head_cols), lambda i, me: (0, 0))],
            scratch_shapes=[pltpu.VMEM((width, 3 * head_cols), BF)],
        ),
        out_shape=[
            jax.ShapeDtypeStruct((length, 3 * head_cols), BF),
            jax.ShapeDtypeStruct((width, 3 * head_cols), BF),
            jax.ShapeDtypeStruct((width, head_cols), BF),
        ],
    )(me, *pieces, first_low, bias[None])


def up_kernel(me_ref, *refs):
    pieces, (low_ref, bias_ref, act_ref, slope_ref, full_ref, scratch) = refs[:8], refs[8:]
    step = pl.program_id(0)

    @pl.when(step == 0)
    def _():
        put_pieces(me_ref[0], pieces, [(scratch, 0, scratch.shape[1])])

    cols = act_ref.shape[1]
    weight = scratch[:, pl.ds(pl.multiple_of(step * cols, cols), cols)]
    full_ref[...] = weight
    for at in range(0, act_ref.shape[0], ROWS):
        rows = slice(at, at + ROWS)
        act, slope = gelu_and_slope(matmul(low_ref[rows, :], weight) + bias_ref[...])
        act_ref[rows, :] = act.astype(BF)
        slope_ref[rows, :] = slope.astype(BF)


def up_of(me, pieces, second_low, bias):
    if len(pieces) == 1:
        act, slope = gelu_and_slope(matmul(second_low, pieces[0]) + bias)
        return act.astype(BF), slope.astype(BF), pieces[0]
    length, width = second_low.shape
    hidden = bias.shape[0]
    cols = pl.BlockSpec((length, COLS), lambda i, me: (0, i))
    return pl.pallas_call(
        up_kernel,
        grid_spec=pltpu.PrefetchScalarGridSpec(
            num_scalar_prefetch=1,
            grid=(hidden // COLS,),
            in_specs=[whole_spec(p) for p in pieces]
            + [whole_spec(second_low), pl.BlockSpec((1, COLS), lambda i, me: (0, i))],
            out_specs=[cols, cols, pl.BlockSpec((width, COLS), lambda i, me: (0, i))],
            scratch_shapes=[pltpu.VMEM((width, hidden), BF)],
        ),
        out_shape=[
            jax.ShapeDtypeStruct((length, hidden), BF),
            jax.ShapeDtypeStruct((length, hidden), BF),
            jax.ShapeDtypeStruct((width, hidden), BF),
        ],
    )(me, *pieces, second_low, bias[None])


def back_kernel(n_steps, me_ref, *refs):
    pieces, refs = refs[:8], refs[8:]
    dy_ref, slope_ref, up_ref, hidden_ref, sum_ref, full_ref, z_ref, scratch, held = refs
    step = pl.program_id(0)

    @pl.when(step == 0)
    def _():
        put_pieces(me_ref[0], pieces, [(scratch, 0, scratch.shape[1])])

    cols = hidden_ref.shape[1]

    @pl.when(step < n_steps)
    def _():
        at = pl.multiple_of(step * cols, cols)
        weight = scratch[pl.ds(at, cols), :]
        full_ref[...] = weight
        total = None
        for start in range(0, dy_ref.shape[0], ROWS):
            rows = slice(start, start + ROWS)
            g_act = dot(dy_ref[rows, :], weight, ((1,), (1,)))
            g_hidden = (g_act * slope_ref[rows, :].astype(F32)).astype(BF)
            hidden_ref[rows, :] = g_hidden
            held[rows, pl.ds(at, cols)] = g_hidden
            part = jnp.sum(g_hidden.astype(F32), axis=0, keepdims=True)
            total = part if total is None else total + part
        sum_ref[...] = total

    @pl.when(step >= n_steps)
    def _():
        z_ref[...] = dot(held[...], up_ref[...], ((1,), (1,))).astype(BF)


def back_of(me, pieces, grad_output, slope, up_full):
    length, width = grad_output.shape
    hidden = slope.shape[1]
    if len(pieces) == 1:
        g_hidden = (dot(grad_output, pieces[0], ((1,), (1,))) * slope.astype(F32)).astype(BF)
        z = dot(g_hidden, up_full, ((1,), (1,))).astype(BF)
        return g_hidden, jnp.sum(g_hidden.astype(F32), axis=0), pieces[0], z
    n_steps, n_late = hidden // COLS, width // ROWS
    early = lambda i: jnp.minimum(i, n_steps - 1)
    late = lambda i: jnp.maximum(i - n_steps, 0)
    cols = pl.BlockSpec((length, COLS), lambda i, me: (0, early(i)))
    return pl.pallas_call(
        functools.partial(back_kernel, n_steps),
        grid_spec=pltpu.PrefetchScalarGridSpec(
            num_scalar_prefetch=1,
            grid=(n_steps + n_late,),
            in_specs=[whole_spec(p) for p in pieces]
            + [whole_spec(grad_output), cols]
            + [pl.BlockSpec((ROWS, hidden), lambda i, me: (late(i), 0))],
            out_specs=[
                cols,
                pl.BlockSpec((1, COLS), lambda i, me: (0, early(i))),
                pl.BlockSpec((COLS, width), lambda i, me: (early(i), 0)),
                pl.BlockSpec((length, ROWS), lambda i, me: (0, late(i))),
            ],
            scratch_shapes=[pltpu.VMEM((hidden, width), BF), pltpu.VMEM((length, hidden), BF)],
        ),
        out_shape=[
            jax.ShapeDtypeStruct((length, hidden), BF),
            jax.ShapeDtypeStruct((1, hidden), F32),
            jax.ShapeDtypeStruct((hidden, width), BF),
            jax.ShapeDtypeStruct((length, width), BF),
        ],
    )(me, *pieces, grad_output, slope, up_full)


def turn_kernel(n, own_blocks, me_ref, *refs):
    own_ref, other_ref, middle_ref, dy_ref, gain_ref = refs[:5]
    weights = refs[5 : 5 + n]
    g_middle_ref, g_attn_ref, g_mixed_ref, sum_ref = refs[5 + n :]
    grad = own_ref[...].astype(F32) + other_ref[...].astype(F32)
    unit, inverse = normed(middle_ref[...])
    g_middle = dy_ref[...].astype(F32) + norm_back(grad, gain_ref[...], unit, inverse)
    if own_blocks:

        @pl.when(pl.program_id(0) // own_blocks == me_ref[0])
        def _():
            g_middle_ref[...] = g_middle

    else:
        g_middle_ref[...] = g_middle
    g_attn = g_middle.astype(BF)
    g_attn_ref[...] = g_attn
    total = None
    for i in range(n):
        width = weights[i].shape[1]
        at = pl.multiple_of(me_ref[1 + i] * width, width)
        part = dot(g_attn_ref[:, pl.ds(at, width)], weights[i][...], ((1,), (1,)))
        total = part if total is None else total + part
    g_mixed_ref[...] = total.astype(BF)
    sums = jnp.concatenate(
        [
            jnp.sum(v, axis=0, keepdims=True)
            for v in (grad * unit, grad, g_attn.astype(F32))
        ]
        + [jnp.zeros((5, grad.shape[1]), F32)],
        axis=0,
    )

    @pl.when(pl.program_id(0) == 0)
    def _():
        sum_ref[...] = sums

    @pl.when(pl.program_id(0) > 0)
    def _():
        sum_ref[...] += sums


def turn_of(me, own, other, middle, grad_output, gain, weights, head_cols, local):
    n, (length, width) = len(weights), middle.shape
    rows = lambda w: pl.BlockSpec((ROWS, w), lambda i, me: (i, 0))
    own_blocks = 0 if local % ROWS else local // ROWS
    kept = rows(width)
    if own_blocks:
        kept = pl.BlockSpec(
            (ROWS, width), lambda i, me: (jnp.clip(i - me[0] * own_blocks, 0, own_blocks - 1), 0)
        )
    return pl.pallas_call(
        functools.partial(turn_kernel, n, own_blocks),
        grid_spec=pltpu.PrefetchScalarGridSpec(
            num_scalar_prefetch=1,
            grid=(length // ROWS,),
            in_specs=[rows(width)] * 4
            + [pl.BlockSpec((1, width), lambda i, me: (0, 0))]
            + [pl.BlockSpec((head_cols, w.shape[1]), lambda i, me: (me[0], 0)) for w in weights],
            out_specs=[kept, rows(width), rows(head_cols)]
            + [pl.BlockSpec((8, width), lambda i, me: (0, 0))],
        ),
        out_shape=[
            jax.ShapeDtypeStruct((local if own_blocks else length, width), F32),
            jax.ShapeDtypeStruct((length, width), BF),
            jax.ShapeDtypeStruct((length, head_cols), BF),
            jax.ShapeDtypeStruct((8, width), F32),
        ],
    )(me, own, other, middle, grad_output, gain[None], *weights)


def make_body(dp, seq):
    def body(
        tokens, segments, cotangent,
        query_weight, key_weight, value_weight, out_weight, up_weight, down_weight,
        query_bias, value_bias, out_bias, up_bias, down_bias,
        first_gain, first_shift, second_gain, second_shift,
    ):
        me_seq = lax.axis_index("seq")
        _, local, width = tokens.shape
        length = segments.shape[1]
        rows = query_weight.shape[0]
        hidden = up_weight.shape[1]
        hidden_rows = down_weight.shape[0]
        head_cols = width // seq
        heads = HEADS // seq
        hidden_cols = hidden // seq

        pairs = heads // 2
        small_params = (
            query_bias, value_bias, out_bias, up_bias, down_bias,
            first_gain, first_shift, second_gain, second_shift,
        )
        small_sizes = [v.shape[0] for v in small_params]
        offsets = [sum(small_sizes[:i]) for i in range(len(small_sizes))]

        def first_columns(s, colour):
            at, half = s * head_cols, head_cols // 2
            span = [pairs * colour // 2, pairs * (colour + 1) // 2] if pairs > 1 else [0, 1]
            parts = [
                w[:, at + p * PAIR : at + (p + 1) * PAIR]
                for p in range(*span)
                for w in (query_weight, key_weight, value_weight)
            ]
            if pairs == 1:
                joined = jnp.concatenate(parts, axis=1)
                parts = [joined[:, colour * 3 * half : (colour + 1) * 3 * half]]
            return parts + [out_weight[:, at + colour * half : at + (colour + 1) * half]]

        quick = seq == 2 and hidden_rows == PAIR and pairs > 1
        if quick:
            own, send, up_mine, up_send = split_weights(
                me_seq, (query_weight, key_weight, value_weight, out_weight), up_weight
            )
            first_own = two_rows(own, trade(send), me_seq)
        else:
            first_own = jnp.stack(
                [jnp.concatenate(first_columns(i, 0) + first_columns(i, 1), axis=1) for i in range(seq)]
            )
            first_own = seq_swap(first_own, seq).reshape(seq * rows, -1)
        q_pieces, mark = gather_blocks(first_own, [3 * head_cols, head_cols], dp)

        total = sum(small_sizes)
        small = sum(
            jnp.pad(v.astype(F32), (at, total - at - size))
            for v, at, size in zip(small_params, offsets, small_sizes)
        )
        small_all = seq_gather(small, seq).reshape(-1, 128)
        small_all = gather_small(small_all, dp).reshape(dp * seq, -1)

        if quick:
            up_own = two_rows(up_mine, trade(up_send), me_seq)
        else:
            up_own = up_weight.reshape(rows, dp, seq, hidden_rows).transpose(2, 0, 1, 3)
            up_own = seq_swap(up_own.reshape(seq, rows, hidden_cols), seq).reshape(seq * rows, -1)
        up_pieces, mark = gather_blocks(up_own, [hidden_cols], dp, mark)
        down_pieces, _ = gather_blocks(down_weight, [width], dp, mark)
        tokens_all = seq_gather(tokens[0], seq).reshape(length, width)
        grad_output = seq_gather(cotangent[0], seq).reshape(length, width)

        def small_of(index):
            return small_all[:, offsets[index] : offsets[index] + small_sizes[index]].reshape(-1)

        (q_shift, v_shift, o_shift, u_shift, d_shift, gain_one, shift_one, gain_two, shift_two) = [
            small_of(i) for i in range(9)
        ]

        def own_pairs(vector):
            return lax.dynamic_slice_in_dim(vector, me_seq * head_cols, head_cols, 0).reshape(pairs, PAIR)

        u_own = pick(u_shift.reshape(dp, seq, hidden_rows), me_seq, 1).reshape(-1)
        qkv_shift = jnp.stack(
            [own_pairs(q_shift), jnp.zeros((pairs, PAIR), F32), own_pairs(v_shift)], axis=1
        ).reshape(-1)

        inputs = tokens_all.astype(F32)
        unit_one, _ = normed(inputs)
        me_dp = lax.axis_index("dp").astype(jnp.int32)[None]
        first_low = (unit_one * gain_one + shift_one).astype(BF)
        unit_low = unit_one.astype(BF)
        ids = (me_seq * heads + jnp.arange(heads) + 1).astype(F32)
        slopes = 2.0 ** (-8.0 * ids / HEADS)
        row, col = segments.reshape(1, length), segments.reshape(length, 1)
        ready = (unit_low, first_low, grad_output, qkv_shift, slopes, row, col, o_shift, u_own, d_shift)
        ready = lax.optimization_barrier(ready)
        unit_low, first_low, grad_output, qkv_shift, slopes, row, col, o_shift, u_own, d_shift = ready
        qkv, qkv_full, out_half = qkv_of(me_dp, q_pieces, first_low, qkv_shift, head_cols)
        if seq == 2:
            out_parts = [out_half, trade(out_half)]
            me_parts = jnp.stack([me_seq, me_seq, 1 - me_seq]).astype(jnp.int32)
        else:
            out_parts = [lax.all_gather(out_half, "seq", axis=1, tiled=True)]
            me_parts = jnp.stack([me_seq, 0]).astype(jnp.int32)

        mixed_own = attend(slopes, row, col, qkv, range(pairs))
        if seq == 2:
            mixed_parts = [mixed_own, trade(mixed_own)]
        else:
            mixed_parts = [lax.all_gather(mixed_own, "seq", axis=1, tiled=True)]
        mixed, middle, second_low = middle_of(
            me_parts, mixed_parts, out_parts, tokens_all, o_shift, gain_two, shift_two
        )
        activated, hidden_slope, up_full = up_of(me_dp, up_pieces, second_low, u_own)

        (down_sum,) = scatter_grads([activated], [grad_output], dp, (0, 1))
        g_hidden, up_bias_sum, down_full, z_own = back_of(
            me_dp, down_pieces, grad_output, hidden_slope, up_full
        )
        (up_sum,) = scatter_grads([second_low], [g_hidden], dp, (0, 1))
        if seq == 2:
            z_other = trade(z_own)
        else:
            z_other = lax.psum(z_own.astype(F32), "seq") - z_own.astype(F32)
        g_middle, g_attn, g_mixed, turn_sums = turn_of(
            me_parts, z_own, z_other, middle, grad_output, gain_two, out_parts, head_cols, local
        )
        groups = [range(pairs // 2), range(pairs // 2, pairs)] if pairs > 1 else [range(pairs)]
        g_qkv = [attend_back(slopes, row, col, qkv, g_mixed, group) for group in groups]
        first_sum, out_sum = scatter_grads([first_low, mixed], [g_qkv[0], g_attn], dp, (0,), head_cols)
        qkv_sums = [first_sum] + [scatter_grads([first_low], [part], dp, (1,))[0] for part in g_qkv[1:]]
        g_qkv = jnp.concatenate(g_qkv, axis=1)
        g_first_part = dot(g_qkv, qkv_full, ((1,), (1,)))
        first_sums = (
            jnp.sum(g_first_part * unit_low.astype(F32), axis=0),
            jnp.sum(g_first_part, axis=0),
        )
        g_first_part = g_first_part.astype(BF)
        g_first = seq_reduce(g_first_part.reshape(seq, local, width), seq, BF)
        unit_own, inverse_own = normed(tokens[0].astype(F32))
        g_middle_own = g_middle
        if g_middle.shape[0] > local:
            g_middle_own = pick(g_middle.reshape(seq, local, width), me_seq, 0)
        input_grad = g_middle_own + norm_back(g_first, gain_one, unit_own, inverse_own)

        late, _ = lax.optimization_barrier((activated, g_qkv))
        lowered = matmul(late, down_full).astype(BF)
        lowered = lowered.reshape(seq, local, width)
        lowered = seq_reduce(lowered, seq, BF)
        middle_own = pick(middle.reshape(seq, local, width), me_seq, 0)
        output = (middle_own + lowered + d_shift).astype(BF)[None]

        def to_rows(total):
            return seq_swap(total.reshape(seq, rows, -1), seq).transpose(1, 0, 2)

        up_rows = to_rows(up_sum).reshape(rows, seq, dp, hidden_rows)
        up_grad = up_rows.transpose(0, 2, 1, 3).reshape(rows, hidden)
        last_rows = to_rows(jnp.concatenate(qkv_sums + [out_sum], axis=1))
        out_grad = last_rows[:, :, 3 * head_cols :].reshape(rows, width)
        qkv_rows = last_rows[:, :, : 3 * head_cols].reshape(rows, seq, pairs, 3, PAIR)
        weight_grads = [qkv_rows[:, :, :, i].reshape(rows, width) for i in range(3)]

        def sums(matrix):
            return jnp.sum(matrix.astype(F32), axis=0)

        mine = jnp.arange(seq) == me_seq

        def heads_only(vector):
            return jnp.where(mine[:, None], vector.reshape(1, -1), 0.0).reshape(-1)

        share = 1.0 / seq
        qkv_columns = sums(g_qkv).reshape(pairs, 3, PAIR)
        up_bias_grad = jnp.where(
            mine[None, :, None], up_bias_sum.reshape(dp, 1, hidden_rows), 0.0
        )
        vectors = [
            heads_only(qkv_columns[:, 0]), heads_only(qkv_columns[:, 2]), turn_sums[2] * share,
            up_bias_grad, sums(cotangent[0]), *first_sums,
            turn_sums[0] * share, turn_sums[1] * share,
        ]
        packed = jnp.concatenate(
            [v.reshape(dp, seq, m) for v, m in zip(vectors, small_sizes)], axis=2
        ).reshape(dp, seq * sum(small_sizes) // 128, 128)
        if boxed(dp):
            small_sum = scatter_far(scatter_near(packed, dp, 0), dp)
        else:
            small_sum = lax.psum_scatter(packed, "dp", scatter_dimension=0, tiled=False)
        small_grad = seq_reduce(small_sum.reshape(seq, -1), seq, F32)
        small_grads = [
            small_grad[offsets[i] : offsets[i] + small_sizes[i]] for i in range(9)
        ]
        return (
            output, input_grad[None], *weight_grads, out_grad, up_grad, down_sum, *small_grads
        )

    return body


def solution(mesh):
    both = ("dp", "seq")
    matrix, vector = P(both, None), P(both)
    dp, seq = mesh.shape["dp"], mesh.shape["seq"]
    layer = make_body(dp, seq)

    return jax.shard_map(
        layer,
        mesh=mesh,
        in_specs=(P("dp", "seq", None), P("dp", None), P("dp", "seq", None))
        + (matrix,) * 6
        + (vector,) * 9,
        out_specs=(P("dp", "seq", None),) * 2 + (matrix,) * 6 + (vector,) * 9,
        check_vma=False,
    )
```
